32 devices in a mesh: seq: 8 (over z, x), tp: 4 (over y, core).
Axes of the slice: x: 2, y: 2, z: 4, core: 2. Of those that a mesh axis runs over, the one named last changes fastest.
Arguments:
- query_heads: bfloat16 [2048, 2048], P('seq', 'tp'), may hold values from -96 to 96
- key_heads: bfloat16 [2048, 2048], P('seq', 'tp'), may hold values from -4 to 4
- value_heads: bfloat16 [2048, 2048], P('seq', 'tp'), may hold values from -6 to 6
- residual: bfloat16 [2048, 4096], P('seq'), may hold values from -64 to 64
- out_weight: bfloat16 [2048, 4096], P('tp'), may hold values from -0.125 to 0.125
- ln_gain: float32 [4096], replicated, may hold values from 0.1 to 1.9
- up_source: bfloat16 [4096, 4096], P(None, 'tp'), may hold values from -0.09375 to 0.09375
- down_source: bfloat16 [4096, 4096], P('tp'), may hold values from -0.09375 to 0.09375
- copy_gain: float32 [4096], P('tp'), may hold values from 0.3 to 3
- neuron_source: int32 [4096], P('tp'), may hold values from 0 to 4095, as said below
- cotangent: bfloat16 [2048, 4096], P('seq'), may hold values from -6 to 6
Outputs:
- encoded: float32 [2048, 4096], P(('seq', 'tp'))
- grad_query: float32 [2048, 2048], P('seq', 'tp')
- grad_key: float32 [2048, 2048], P('seq', 'tp')
- grad_value: float32 [2048, 2048], P('seq', 'tp')
- grad_residual: float32 [2048, 4096], P('seq', 'tp')
The draws below stay inside these ranges and needn't reach their ends.
Inputs may be any that keep to these rules, and one draw needn't show every extreme that they name: Added neuron j splits a source neuron of its own group: neuron_source[j] // 1024 == j // 1024.
All inputs are finite; a program needn't handle non-finite values.
Results may differ from the reference program's by a relative error of at most 0.035.
Values may be sent and summed in bfloat16 or wider, within the bound.
A program may use at most 128 MiB of HBM per device.

```python
import math
import jax
import jax.numpy as jnp
from jax import lax

D = 4096
HEADS = 16
HEAD_DIM = 128
FF_SRC = 4096
FF_COPY = 4096
TOK_DEV = 256
TOKENS = 2048
SRC_SHARD = 1024
COPY_SHARD = 1024
N_SEQ = 8
N_TP = 4


def query_key_pair(key):
    head_width = HEADS * HEAD_DIM
    query_base = jax.random.truncated_normal(jax.random.fold_in(key, 11), -4.0, 4.0, (TOKENS, head_width), jnp.float32)
    key_base = jax.random.truncated_normal(jax.random.fold_in(key, 12), -4.0, 4.0, (TOKENS, head_width), jnp.float32)
    return (query_base, key_base)


def draw_query_heads(key, part):
    return query_key_pair(key)[0].astype(jnp.bfloat16)


def draw_key_heads(key, part):
    return query_key_pair(key)[1].astype(jnp.bfloat16)


def draw_residual(key, part):
    base = jax.random.truncated_normal(jax.random.fold_in(key, 21), -5.0, 5.0, (TOKENS, D), jnp.float32)
    column_scale = jnp.exp(jax.random.uniform(jax.random.fold_in(key, 22), (1, D), jnp.float32, math.log(0.3), math.log(3.0)))
    return (base * column_scale).astype(jnp.bfloat16)


def draw_neuron_source(key, part):
    local_pick = jax.random.randint(key, (FF_COPY,), 0, SRC_SHARD, dtype=jnp.int32)
    owner_group = jnp.arange(FF_COPY, dtype=jnp.int32) // COPY_SHARD
    picked = owner_group * SRC_SHARD + local_pick
    return picked.at[0].set(0).at[FF_COPY - 1].set(FF_SRC - 1)


def shard_levels(own_key, extent, pieces, low, largest):
    level = 1.0
    for position, parts in pieces:
        steps = jax.random.uniform(jax.random.fold_in(jax.random.fold_in(own_key, 6), position), (parts,), jnp.float32, low / len(pieces), largest / len(pieces))
        level = level * jnp.repeat(jnp.exp(steps), extent[position] // parts).reshape((-1,) + (1,) * (len(extent) - 1 - position))
    return level


def noise(own_key, dims, width, limit, cuts=(), held_as=jnp.bfloat16):
    values = jax.random.normal(own_key, dims, jnp.float32) * width
    if len(cuts) > 0:
        values = shard_levels(own_key, dims, cuts, -0.22, 0.18) * values
    return jnp.clip(values, min=-limit, max=limit).astype(held_as)


def setup_inputs(seed: int = 0) -> dict:
    seeds = jax.random.split(jax.random.key(seed), 12)
    query_heads = draw_query_heads(jax.random.fold_in(seeds[11], 71), 0)
    key_heads = draw_key_heads(jax.random.fold_in(seeds[11], 71), 0)
    value_heads = noise(seeds[2], (TOKENS, HEADS * HEAD_DIM), 1.0, 6.0, ((0, 8), (1, 4)))
    residual = draw_residual(jax.random.fold_in(seeds[11], 71), 0)
    out_weight = noise(seeds[4], (HEADS * HEAD_DIM, D), (HEADS * HEAD_DIM) ** -0.5, 0.125, ((0, 4),))
    ln_gain = jnp.clip(1.0 + 0.18 * jax.random.normal(seeds[5], (D,), jnp.float32), 0.1, 1.9)
    up_source = noise(seeds[6], (D, FF_SRC), D ** -0.5, 0.09375, ((1, 4),))
    down_source = noise(seeds[7], (FF_SRC, D), FF_SRC ** -0.5, 0.09375, ((0, 4),))
    copy_gain = jnp.clip(jnp.exp(math.log(3.0) - 2.3025851 * jax.random.uniform(seeds[8], (FF_COPY,), jnp.float32) ** shard_levels(seeds[8], (FF_COPY,), ((0, 4),), -0.2, 0.2)), 0.3, 3.0)
    neuron_source = draw_neuron_source(jax.random.fold_in(seeds[11], 71), 0)
    cotangent = noise(seeds[10], (TOKENS, D), 1.0, 6.0, ((0, 8),))
    return dict(query_heads=query_heads, key_heads=key_heads, value_heads=value_heads, residual=residual, out_weight=out_weight, ln_gain=ln_gain, up_source=up_source, down_source=down_source, copy_gain=copy_gain, neuron_source=neuron_source, cotangent=cotangent)


epsilon = 1e-05

def gelu_slope(inputs):
    output, pull_back = jax.vjp(jax.nn.gelu, inputs)
    return (output, pull_back(jnp.ones_like(inputs))[0])

def layer_norm_rows(stream):
    centered = stream - lax.optimization_barrier(jnp.mean(stream, axis=-1, keepdims=True))
    row_sigma = jnp.sqrt(lax.optimization_barrier(jnp.mean(centered * centered, axis=-1, keepdims=True)) + epsilon)
    return (centered / row_sigma, row_sigma)

def reference(query_heads, key_heads, value_heads, residual, out_weight, ln_gain, up_source, down_source, copy_gain, neuron_source, cotangent):
    head_width = HEADS * HEAD_DIM
    group_heads = head_width // N_TP
    group_src = FF_SRC // N_TP
    score_scale = 1.0 / math.sqrt(HEAD_DIM)
    margin = 2 * TOK_DEV
    span_rows = 5 * TOK_DEV

    def pad_rows(array):
        return jnp.pad(array.reshape(TOKENS, HEADS, HEAD_DIM), ((margin, margin), (0, 0), (0, 0)))
    key_pad = pad_rows(key_heads)
    value_pad = pad_rows(value_heads)

    def block_view(block):
        row_start = (block * TOK_DEV).astype(jnp.int32)
        queries = lax.dynamic_slice_in_dim(query_heads, row_start, TOK_DEV, 0).reshape(TOK_DEV, HEADS, HEAD_DIM)
        keys_near = lax.dynamic_slice_in_dim(key_pad, row_start, span_rows, 0)
        values_near = lax.dynamic_slice_in_dim(value_pad, row_start, span_rows, 0)
        block_of = block + jnp.arange(span_rows, dtype=jnp.int32) // TOK_DEV - 2
        is_valid = (block_of >= 0) & (block_of < N_SEQ)
        scores = jnp.einsum('rhd,khd->hrk', queries.astype(jnp.float32), keys_near.astype(jnp.float32)) * score_scale
        scores = jnp.where(is_valid[None, None, :], scores, -jnp.inf)
        row_top = lax.optimization_barrier(jnp.max(scores, axis=-1, keepdims=True))
        exp_scores = jnp.exp(scores - row_top)
        attn_probs = exp_scores / lax.optimization_barrier(jnp.sum(exp_scores, axis=-1, keepdims=True))
        return (row_start, queries, keys_near, values_near, attn_probs)

    def forward_block(block):
        row_start, queries, keys_near, values_near, attn_probs = block_view(block)
        attn_low = attn_probs.astype(jnp.bfloat16)
        return jnp.einsum('hrk,khd->rhd', attn_low.astype(jnp.float32), values_near.astype(jnp.float32)).astype(jnp.bfloat16)
    block_ids = jnp.arange(N_SEQ, dtype=jnp.int32)
    attended = lax.map(forward_block, block_ids).reshape(TOKENS, head_width)
    mixed = jnp.zeros((TOKENS, D), jnp.float32)
    for group_index in range(N_TP):
        head_cols = slice(group_index * group_heads, (group_index + 1) * group_heads)
        head_part = jnp.dot(attended[:, head_cols], out_weight[head_cols], preferred_element_type=jnp.float32).astype(jnp.bfloat16)
        mixed = mixed + head_part.astype(jnp.float32)
    stream = residual.astype(jnp.float32) + mixed
    unit_rows, row_sigma = layer_norm_rows(stream)
    normed_full = unit_rows * ln_gain
    normed = normed_full.astype(jnp.bfloat16)
    hidden_in = jnp.dot(normed, up_source, preferred_element_type=jnp.float32)
    counts = jnp.ones((FF_SRC,), jnp.float32).at[neuron_source].add(1.0)
    copies_in = hidden_in[:, neuron_source] * copy_gain
    act_src, slope_src = gelu_slope(hidden_in)
    act_copy, slope_copy = gelu_slope(copies_in)
    merged = (act_src.at[:, neuron_source].add(act_copy) / counts).astype(jnp.bfloat16)
    ffn_total = jnp.zeros((TOKENS, D), jnp.float32)
    for group_index in range(N_TP):
        src_cols = slice(group_index * group_src, (group_index + 1) * group_src)
        ffn_part = jnp.dot(merged[:, src_cols], down_source[src_cols], preferred_element_type=jnp.float32).astype(jnp.bfloat16)
        ffn_total = ffn_total + ffn_part.astype(jnp.float32)
    encoded = normed_full + ffn_total
    grad_merged = jnp.dot(cotangent, down_source.T, preferred_element_type=jnp.float32)
    inverse = 1.0 / counts
    grad_src = grad_merged * inverse * slope_src
    grad_copy = grad_merged[:, neuron_source] * inverse[neuron_source] * slope_copy
    grad_hidden = grad_src.at[:, neuron_source].add(grad_copy * copy_gain).astype(jnp.bfloat16)
    grad_normed = cotangent.astype(jnp.float32)
    for group_index in range(N_TP):
        src_cols = slice(group_index * group_src, (group_index + 1) * group_src)
        back_part = jnp.dot(grad_hidden[:, src_cols], up_source[:, src_cols].T, preferred_element_type=jnp.float32).astype(jnp.bfloat16)
        grad_normed = grad_normed + back_part.astype(jnp.float32)
    scaled = grad_normed * ln_gain
    grad_residual = (scaled - lax.optimization_barrier(jnp.mean(scaled, axis=-1, keepdims=True)) - unit_rows * lax.optimization_barrier(jnp.mean(scaled * unit_rows, axis=-1, keepdims=True))) / row_sigma
    grad_low = grad_residual.astype(jnp.bfloat16)
    grad_attended = jnp.dot(grad_low, out_weight.T, preferred_element_type=jnp.float32).astype(jnp.bfloat16)
    grad_start = jnp.zeros((TOKENS + 2 * margin, HEADS, HEAD_DIM), jnp.float32)

    def backward_block(carry, block):
        key_acc, value_acc = carry
        row_start, queries, keys_near, values_near, attn_probs = block_view(block)
        attn_low = attn_probs.astype(jnp.bfloat16)
        out_block = lax.dynamic_slice_in_dim(attended, row_start, TOK_DEV, 0).reshape(TOK_DEV, HEADS, HEAD_DIM)
        grad_block = lax.dynamic_slice_in_dim(grad_attended, row_start, TOK_DEV, 0).reshape(TOK_DEV, HEADS, HEAD_DIM)
        row_delta = lax.optimization_barrier(jnp.sum(grad_block.astype(jnp.float32) * out_block.astype(jnp.float32), axis=-1)).T
        grad_probs = jnp.einsum('rhd,khd->hrk', grad_block.astype(jnp.float32), values_near.astype(jnp.float32))
        grad_scores = (attn_probs * (grad_probs - row_delta[:, :, None])).astype(jnp.bfloat16)
        grad_q = score_scale * jnp.einsum('hrk,khd->rhd', grad_scores.astype(jnp.float32), keys_near.astype(jnp.float32))
        grad_k = score_scale * jnp.einsum('hrk,rhd->khd', grad_scores.astype(jnp.float32), queries.astype(jnp.float32))
        grad_v = jnp.einsum('hrk,rhd->khd', attn_low.astype(jnp.float32), grad_block.astype(jnp.float32))
        key_acc = lax.dynamic_update_slice_in_dim(key_acc, lax.dynamic_slice_in_dim(key_acc, row_start, span_rows, 0) + grad_k, row_start, 0)
        value_acc = lax.dynamic_update_slice_in_dim(value_acc, lax.dynamic_slice_in_dim(value_acc, row_start, span_rows, 0) + grad_v, row_start, 0)
        return ((key_acc, value_acc), grad_q)
    (key_acc, value_acc), grad_q = lax.scan(backward_block, (grad_start, grad_start), block_ids)
    grad_query = grad_q.reshape(TOKENS, head_width)
    grad_key = key_acc[margin:margin + TOKENS].reshape(TOKENS, head_width)
    grad_value = value_acc[margin:margin + TOKENS].reshape(TOKENS, head_width)
    return (encoded, grad_query, grad_key, grad_value, grad_residual)
```

```python
import functools
import math

import jax
import jax.numpy as jnp
from jax import lax
from jax.experimental import pallas as pl
from jax.experimental.pallas import tpu as pltpu
from jax.sharding import PartitionSpec as P

HEAD_DIM = 128
OFFSETS = (-2, -1, 1, 2)
OWN = 4
HALVES = 2
PIECES = 4
TILE = 512
epsilon = 1e-05
MESH = pl.DeviceIdType.MESH
VM = pltpu.VMEM
F32 = jnp.float32
BF16 = jnp.bfloat16
SCALE = 1.0 / math.sqrt(HEAD_DIM)


def dot_nn(a, b):
    return jnp.dot(a, b, preferred_element_type=F32)


def dot_nt(a, b):
    return lax.dot_general(a, b, (((1,), (1,)), ((), ())), preferred_element_type=F32)


def dot_tn(a, b):
    return lax.dot_general(a, b, (((0,), (0,)), ((), ())), preferred_element_type=F32)


def remote(src, dst, send, recv, **where):
    return pltpu.make_async_remote_copy(
        src_ref=src, dst_ref=dst, send_sem=send, recv_sem=recv, device_id=where, device_id_type=MESH
    )


def gelu_slope(v):
    rate = math.sqrt(2.0 / math.pi)
    square = v * v
    bend = jnp.tanh(rate * v * (1.0 + 0.044715 * square))
    level = 0.5 * (1.0 + bend)
    slope = level + (0.5 * rate) * v * (1.0 - bend * bend) * (1.0 + 0.134145 * square)
    return v * level, slope


class Blocks:
    def __init__(self, count):
        self.count = count
        self.place = lax.axis_index("seq")
        self.even = lax.rem(self.place, 2) == 0

    def there(self, offset):
        other = self.place + offset
        return (other >= 0) & (other < self.count)

    def greet(self, barrier):
        for offset in OFFSETS:
            @pl.when(self.there(offset))
            def _():
                pl.semaphore_signal(
                    barrier, inc=1, device_id={"seq": self.place + offset}, device_id_type=MESH
                )

    def greeted(self, barrier, more):
        peers = sum(self.there(offset).astype(jnp.int32) for offset in OFFSETS)
        pl.semaphore_wait(barrier, peers + more)

    def copy(self, src, window, send, recv, index, slot):
        return remote(
            src, window(slot), send.at[index], recv.at[slot], seq=self.place + OFFSETS[index]
        )

    def send(self, src, window, send, recv):
        for index, offset in enumerate(OFFSETS):
            @pl.when(self.there(offset))
            def _():
                self.copy(src, window, send, recv, index, 3 - index).start()

    def arrive(self, src, window, send, recv):
        for index, offset in enumerate(OFFSETS):
            @pl.when(self.there(offset))
            def _():
                self.copy(src, window, send, recv, index, index).wait_recv()

    def left(self, src, window, send, recv):
        for index, offset in enumerate(OFFSETS):
            @pl.when(self.there(offset))
            def _():
                self.copy(src, window, send, recv, index, 3 - index).wait_send()

    def clear(self, window):
        for index, offset in enumerate(OFFSETS):
            @pl.when(jnp.logical_not(self.there(offset)))
            def _():
                ref = window(index)
                ref[...] = jnp.zeros(ref.shape, ref.dtype)


class Halo:
    def __init__(self, blocks, buf, send, recv, fwd, across):
        self.blocks, self.buf, self.send_sem, self.recv_sem, self.fwd = blocks, buf, send, recv, fwd
        self.across = across

    def window(self, slot):
        return self.buf.at[slot]

    def hops(self, even):
        return (0, 2 if even else 1, 3)

    def both(self, act):
        for even in (True, False):
            @pl.when(self.blocks.even == even)
            def _():
                act(even)

    def copy(self, index, slot):
        return self.blocks.copy(
            self.buf.at[OWN], self.window, self.send_sem, self.recv_sem, index, slot
        )

    def start(self):
        def act(even):
            for index in self.hops(even):
                @pl.when(self.blocks.there(OFFSETS[index]))
                def _():
                    self.copy(index, 3 - index).start()

        self.both(act)

    def passing(self, even):
        if self.across:
            return (3, 1, 2, 2) if even else (0, -1, 1, -2)
        return (2, 2, 1, 2) if even else (1, -2, 2, -2)

    def pass_copy(self, even):
        slot, to, there, need = self.passing(even)
        return remote(
            self.buf.at[slot], self.buf.at[there], self.fwd, self.recv_sem.at[there],
            seq=self.blocks.place + to,
        ), need

    def relay(self):
        def act(even):
            slot = self.passing(even)[0]
            copy, need = self.pass_copy(even)

            @pl.when(self.blocks.there(OFFSETS[slot]))
            def _():
                self.copy(slot, slot).wait_recv()

            @pl.when(self.blocks.there(need))
            def _():
                copy.start()

        self.both(act)

    def arrive(self):
        def act(even):
            for index in range(4):
                if index != self.passing(even)[0]:
                    @pl.when(self.blocks.there(OFFSETS[index]))
                    def _():
                        self.copy(index, index).wait_recv()

        self.both(act)

    def left(self):
        def act(even):
            for index in self.hops(even):
                @pl.when(self.blocks.there(OFFSETS[index]))
                def _():
                    self.copy(index, 3 - index).wait_send()
            copy, need = self.pass_copy(even)

            @pl.when(self.blocks.there(need))
            def _():
                copy.wait_send()

        self.both(act)


class Group:
    def __init__(self):
        me = lax.axis_index("tp")
        chip, core = lax.div(me, 2), lax.rem(me, 2)
        self.me = me
        self.sibling = chip * 2 + 1 - core
        self.far = (1 - chip) * 2 + core
        self.across = (1 - chip) * 2 + 1 - core

    def greet(self, barrier):
        for other in (self.sibling, self.far):
            pl.semaphore_signal(barrier, inc=1, device_id={"tp": other}, device_id_type=MESH)


def layer_kernel(
    count,
    q_hbm, k_hbm, v_hbm, res_hbm, w_hbm, gain_hbm, up_hbm, down_hbm, cg_hbm, src_hbm, cot_hbm,
    enc_ref, gq_ref, gk_ref, gv_ref, gres_ref,
    w, up, down, pick, cot, res, gain, cg_row, src_row,
    kbuf, vbuf, q, qwin, do, dwin, prob, probt, att, stat, swin, dcol, drow, twin,
    scaled, gcp, hid, actc, gcb, merged, gh, gacc, inv, unit, sigma, full1, full2,
    sb, rb, mine, s2b, r2b,
    load_sem, slab_sem, ks, kr, kf, vs, vr, vf, qs, qr, ts, tr, ds_, dr, es, er,
    s1, r1, s2, r2, ags, agr,
):
    blocks, group = Blocks(count), Group()
    groups, rows, width = sb.shape[2], s2b.shape[3], s2b.shape[4]
    half = groups * rows
    own = HALVES * rows
    heads = kbuf.shape[0]
    tok = HALVES * half
    src = up.shape[1]
    depth = src // PIECES

    def cols(cg):
        return pl.ds(pl.multiple_of(cg * width, width), width)

    def slab(owner):
        return pl.ds(pl.multiple_of(owner * rows, rows), rows)

    loads = {}

    def load(name, source, target, sem):
        loads.setdefault(name, []).append(pltpu.make_async_copy(source, target, sem))

    def arrived(name):
        for copy in loads[name]:
            copy.wait()

    for h in range(heads):
        span = pl.ds(h * HEAD_DIM, HEAD_DIM)
        load("k", k_hbm.at[:, span], kbuf.at[h, OWN], load_sem.at[2 * h])
        load("v", v_hbm.at[:, span], vbuf.at[h, OWN], load_sem.at[2 * h + 1])
    at = 2 * heads
    load("src", src_hbm, src_row, load_sem.at[at])
    load("cg", cg_hbm, cg_row, load_sem.at[at + 1])
    load("gain", gain_hbm, gain, load_sem.at[at + 2])
    load("w", w_hbm, w, load_sem.at[at + 3])
    load("up", up_hbm, up, load_sem.at[at + 4])
    load("res", res_hbm.at[pl.ds(pl.multiple_of(group.me * own, own), own)], res, load_sem.at[at + 5])
    at = at + 6
    for i in range(PIECES):
        span = pl.ds(i * depth, depth)
        load("down%d" % i, down_hbm.at[span], down.at[span], load_sem.at[at + i])
    for i in range(groups * HALVES):
        owner, h = divmod(i, HALVES)
        source = pl.ds(owner * own + h * rows, rows)
        load("cot", cot_hbm.at[source], cot.at[h, pl.ds(owner * rows, rows)], slab_sem.at[0, i])
        load("q", q_hbm.at[source], q.at[h, pl.ds(owner * rows, rows)], slab_sem.at[1, i])
    order = ["k", "v", "src", "cg", "q", "cot"] + ["down%d" % i for i in range(PIECES)]
    for name in order + ["gain", "w", "res", "up"]:
        for copy in loads[name]:
            copy.start()

    barrier = pltpu.get_barrier_semaphore()
    group.greet(barrier)
    blocks.greet(barrier)
    khalo = [Halo(blocks, kbuf.at[h], ks.at[h], kr.at[h], kf.at[h], True) for h in range(heads)]
    vhalo = [Halo(blocks, vbuf.at[h], vs.at[h], vr.at[h], vf.at[h], False) for h in range(heads)]
    arrived("k")
    arrived("v")
    blocks.greeted(barrier, 2)
    for h in range(heads):
        khalo[h].start()
        vhalo[h].start()

    def kslots(index):
        return kbuf.at[:, index]

    def vslots(index):
        return vbuf.at[:, index]

    blocks.clear(kslots)
    blocks.clear(vslots)
    for h in range(HALVES):
        blocks.clear(lambda index: qwin.at[h, index])
        blocks.clear(lambda index: dwin.at[h, index])
        blocks.clear(lambda index: twin.at[h, index])
    blocks.clear(lambda index: swin.at[index])

    arrived("src")
    arrived("cg")
    local = src_row[...] - group.me * src

    @pl.loop(0, PIECES)
    def _(i):
        place = lax.broadcasted_iota(jnp.int32, (depth, local.shape[1]), 0) + i * depth
        pick[pl.ds(pl.multiple_of(i * depth, depth), depth), :] = (
            jnp.where(place == local, 1.0, 0.0).astype(BF16)
        )

    ones = jnp.ones((16, local.shape[1]), BF16)
    inv[...] = 1.0 / (1.0 + dot_nt(ones, pick[...])[:8])

    def merged_grad(i):
        arrived("down%d" % i)
        span = slice(i * depth, (i + 1) * depth)
        for h in range(HALVES):
            scaled[h, :, span] = dot_nt(cot[h], down[span]) * inv[:1, span]

    stat_lane = lax.broadcasted_iota(jnp.int32, (tok, HEAD_DIM), 1)
    bias = jnp.concatenate(
        [
            jnp.full((1, tok), jnp.where(blocks.there(offset), 0.0, -1e30).astype(F32))
            for offset in OFFSETS
        ]
        + [jnp.zeros((1, tok), F32)],
        axis=1,
    )

    def attend(h, stats):
        khalo[h].arrive()
        vhalo[h].arrive()
        span = slice(h * HEAD_DIM, (h + 1) * HEAD_DIM)
        tops, inverses = [], []
        for part in range(HALVES):
            keys = kbuf[h].reshape(5 * tok, HEAD_DIM)
            scores = dot_nt(q[part, :, span], keys) * SCALE + bias
            top = jnp.max(scores, axis=1, keepdims=True)
            exps = jnp.exp(scores - top)
            inverse = 1.0 / jnp.sum(exps, axis=1, keepdims=True)
            low = (exps * inverse).astype(BF16)
            prob[h, part] = low
            att[part, :, span] = dot_nn(low, vbuf[h].reshape(5 * tok, HEAD_DIM)).astype(BF16)
            tops.append(top)
            inverses.append(inverse)
        stats = jnp.where(stat_lane == h, jnp.concatenate(tops, axis=0), stats)
        return jnp.where(stat_lane == heads + h, jnp.concatenate(inverses, axis=0), stats)

    def relay(h):
        khalo[h].relay()
        vhalo[h].relay()

    stats = jnp.zeros((tok, HEAD_DIM), F32)
    relay(0)
    arrived("cot")
    merged_grad(0)
    relay(1)
    merged_grad(1)
    arrived("q")
    stats = attend(0, stats)
    relay(2)
    merged_grad(2)
    merged_grad(3)
    stats = attend(1, stats)
    relay(3)
    for h in range(HALVES):
        gcp[h] = dot_nn(scaled[h].astype(BF16), pick[...]) * cg_row[...]
    for h in range(2, heads):
        stats = attend(h, stats)
    stat[...] = jnp.transpose(stats)[: 2 * heads]

    def qwindow(h):
        return lambda slot: qwin.at[h, slot]

    def dwindow(h):
        return lambda slot: dwin.at[h, slot]

    def twindow(h):
        return lambda slot: twin.at[h, slot]

    def swindow(slot):
        return swin.at[slot]

    def first(stage, h, cg):
        return remote(
            sb.at[stage, h, cg], rb.at[stage, h, cg], s1.at[stage, h, cg], r1.at[stage, h, cg],
            tp=group.sibling,
        )

    def second(stage, h, cg):
        return remote(
            s2b.at[stage, h, cg], r2b.at[stage, h, cg], s2.at[stage, h, cg], r2.at[stage, h, cg],
            tp=group.far,
        )

    def hop1(stage, h, cg, lhs_ref, product):
        lhs = jnp.concatenate(
            [
                lhs_ref[h, slab(o), :]
                for o in (group.across, group.sibling, group.far, group.me)
            ],
            axis=0,
        )
        part = product(lhs, cg).astype(BF16)
        sb[stage, h, cg] = part[: 2 * rows]
        mine[stage, h, cg] = part[2 * rows :]
        first(stage, h, cg).start()

    def hop2(stage, h, cg):
        first(stage, h, cg).wait_recv()
        s2b[stage, h, cg] = (
            mine[stage, h, cg, :rows].astype(F32) + rb[stage, h, cg, :rows].astype(F32)
        ).astype(BF16)
        second(stage, h, cg).start()

    def total(stage, h, cg):
        return (
            mine[stage, h, cg, rows:].astype(F32)
            + rb[stage, h, cg, rows:].astype(F32)
            + r2b[stage, h, cg].astype(F32)
        )

    def spread(stage, full, h, cg, kind):
        owner = group.far if kind == 2 else group.me
        to = group.far if kind == 0 else group.sibling
        ref = full.at[h, cg, slab(owner)]
        return remote(ref, ref, ags.at[stage, h, cg, kind], agr.at[stage, h, cg, kind], tp=to)

    def spread_own(stage, full, h):
        for cg in range(groups):
            spread(stage, full, h, cg, 0).start()
            spread(stage, full, h, cg, 1).start()

    def pass_on(stage, full, h, cg):
        spread(stage, full, h, cg, 0).wait_recv()
        spread(stage, full, h, cg, 2).start()

    def gather(stage, full, h, use):
        pass_on(stage, full, h, 0)

        @pl.loop(0, groups)
        def _(cg):
            @pl.when(cg + 1 < groups)
            def _():
                pass_on(stage, full, h, cg + 1)

            spread(stage, full, h, cg, 1).wait_recv()
            spread(stage, full, h, cg, 2).wait_recv()
            use(cg)

    def out_product(lhs, cg):
        return dot_nn(lhs, w[:, cols(cg)])

    def back_product(lhs, cg):
        return dot_nt(lhs, up[cols(cg), :])

    def ffn_product(lhs, cg):
        return dot_nn(lhs, down[:, cols(cg)])

    def reduce_all(stage, lhs_ref, product):
        for h in range(HALVES):
            @pl.loop(0, groups)
            def _(cg):
                hop1(stage, h, cg, lhs_ref, product)
                if h > 0:
                    hop2(stage, h - 1, cg)

        @pl.loop(0, groups)
        def _(cg):
            hop2(stage, HALVES - 1, cg)

    arrived("w")
    reduce_all(0, att, out_product)
    for h in range(HALVES):
        blocks.send(q.at[h], qwindow(h), qs.at[h], qr.at[h])
    blocks.send(stat, swindow, ts, tr)

    arrived("res")
    arrived("gain")
    scale = 1.0 / (groups * width)
    for h in range(HALVES):
        part = slice(h * rows, (h + 1) * rows)
        sums = jnp.zeros((rows, 1), F32)
        for cg in range(groups):
            second(0, h, cg).wait_recv()
            stream = res[part, cg * width : (cg + 1) * width].astype(F32) + total(0, h, cg)
            unit[h, cg] = stream
            sums = sums + jnp.sum(stream, axis=1, keepdims=True)
        mean = sums * scale
        squares = jnp.zeros((rows, 1), F32)
        for cg in range(groups):
            centered = unit[h, cg] - mean
            squares = squares + jnp.sum(centered * centered, axis=1, keepdims=True)
        deviation = jnp.sqrt(squares * scale + epsilon)
        sigma[h] = jnp.broadcast_to(deviation, (rows, HEAD_DIM))
        for cg in range(groups):
            level = (unit[h, cg] - mean) / deviation
            unit[h, cg] = level
            full1[h, cg, slab(group.me), :] = (
                level * gain[:, cg * width : (cg + 1) * width]
            ).astype(BF16)
        spread_own(0, full1, h)

    blocks.arrive(stat, swindow, ts, tr)
    for h in range(HALVES):
        blocks.arrive(q.at[h], qwindow(h), qs.at[h], qr.at[h])

    def row_of(ref, lead, line):
        return jnp.concatenate([lead(ref, slot)[line : line + 1, :] for slot in range(4)], axis=1)

    for part in range(HALVES):
        for h in range(heads):
            span = slice(h * HEAD_DIM, (h + 1) * HEAD_DIM)
            queries = qwin[part, :, :, span].reshape(4 * half, HEAD_DIM)
            lanes = slice(part * half, (part + 1) * half)
            top = jnp.concatenate([swin[s, h : h + 1, lanes] for s in range(4)], axis=1)
            inverse = jnp.concatenate(
                [swin[s, heads + h : heads + h + 1, lanes] for s in range(4)], axis=1
            )
            probt[h, part] = (
                jnp.exp(dot_nt(kbuf[h, OWN], queries) * SCALE - top) * inverse
            ).astype(BF16)

    arrived("up")
    tiles = src // TILE
    for h in range(HALVES):
        hid[h] = jnp.zeros(hid.shape[1:], F32)

        def use_hidden(cg):
            hid[h] += dot_nn(full1[h, cg], up[cols(cg), :])

        gather(0, full1, h, use_hidden)

        @pl.loop(0, tiles)
        def _(t):
            span = pl.ds(pl.multiple_of(t * TILE, TILE), TILE)
            copies = dot_nn(hid[h].astype(BF16), pick[:, span]) * cg_row[:, span]
            act, slope = gelu_slope(copies)
            actc[h, :, span] = act.astype(BF16)
            gcb[:, span] = (gcp[h, :, span] * slope).astype(BF16)

        @pl.loop(0, tiles)
        def _(t):
            span = pl.ds(pl.multiple_of(t * TILE, TILE), TILE)
            act, slope = gelu_slope(hid[h, :, span])
            hid[h, :, span] = act
            gh[h, :, span] = (
                scaled[h, :, span] * slope + dot_nt(gcb[...], pick[span, :])
            ).astype(BF16)

        @pl.loop(0, groups)
        def _(cg):
            hop1(1, h, cg, gh, back_product)

        @pl.loop(0, groups)
        def _(cg):
            hop2(1, h, cg)

    for h in range(HALVES):
        @pl.loop(0, tiles)
        def _(t):
            span = pl.ds(pl.multiple_of(t * TILE, TILE), TILE)
            merged[h, :, span] = (
                (hid[h, :, span] + dot_nt(actc[h], pick[span, :])) * inv[:1, span]
            ).astype(BF16)

        @pl.loop(0, groups)
        def _(cg):
            hop1(2, h, cg, merged, ffn_product)

    for h in range(HALVES):
        sums = jnp.zeros((rows, 1), F32)
        along = jnp.zeros((rows, 1), F32)
        pieces = []
        for cg in range(groups):
            span = slice(cg * width, (cg + 1) * width)
            second(1, h, cg).wait_recv()
            grad = cot[h, slab(group.me), span].astype(F32) + total(1, h, cg)
            graded = grad * gain[:, span]
            pieces.append(graded)
            sums = sums + jnp.sum(graded, axis=1, keepdims=True)
            along = along + jnp.sum(graded * unit[h, cg], axis=1, keepdims=True)
        for cg in range(groups):
            full2[h, cg, slab(group.me), :] = (
                (pieces[cg] - sums * scale - unit[h, cg] * (along * scale)) / sigma[h, :, :1]
            ).astype(BF16)
        spread_own(1, full2, h)

    for h in range(HALVES):
        @pl.loop(0, groups)
        def _(cg):
            hop2(2, h, cg)

    lane = lax.broadcasted_iota(jnp.int32, (half, HEAD_DIM), 1)

    def query_side(part):
        for h in range(heads):
            span = slice(h * HEAD_DIM, (h + 1) * HEAD_DIM)
            grads = do[part, :, span]
            chance = prob[h, part]
            slope = (
                chance.astype(F32)
                * (
                    dot_nt(grads, vbuf[h].reshape(5 * tok, HEAD_DIM))
                    - dcol[part, :, h : h + 1]
                )
            ).astype(BF16)
            gq_ref[part, :, span] = dot_nn(slope, kbuf[h].reshape(5 * tok, HEAD_DIM)) * SCALE
            near = slice(OWN * tok, (OWN + 1) * tok)
            grad_k = dot_tn(slope[:, near], q[part, :, span]) * SCALE
            grad_v = dot_tn(chance[:, near], grads)
            if part == 0:
                gk_ref[:, span] = grad_k
                gv_ref[:, span] = grad_v
            else:
                gk_ref[:, span] += grad_k
                gv_ref[:, span] += grad_v

    def key_side(part):
        blocks.arrive(do.at[part], dwindow(part), ds_.at[part], dr.at[part])
        blocks.arrive(drow.at[part], twindow(part), es.at[part], er.at[part])
        for h in range(heads):
            span = slice(h * HEAD_DIM, (h + 1) * HEAD_DIM)
            queries = qwin[part, :, :, span].reshape(4 * half, HEAD_DIM)
            grads = dwin[part, :, :, span].reshape(4 * half, HEAD_DIM)
            delta = jnp.concatenate([twin[part, s, h : h + 1, :] for s in range(4)], axis=1)
            chance = probt[h, part]
            slope = (chance.astype(F32) * (dot_nt(vbuf[h, OWN], grads) - delta)).astype(BF16)
            gv_ref[:, span] += dot_nn(chance, grads)
            gk_ref[:, span] += dot_nn(slope, queries) * SCALE

    for part in range(HALVES):
        gacc[...] = jnp.zeros(gacc.shape, F32)

        def use_low(cg):
            gacc[...] += dot_nt(full2[part, cg], w[:, cols(cg)])

        gather(1, full2, part, use_low)
        grad_att = gacc[...].astype(BF16)
        do[part] = grad_att
        blocks.send(do.at[part], dwindow(part), ds_.at[part], dr.at[part])
        deltas = jnp.zeros((half, HEAD_DIM), F32)
        for h in range(heads):
            span = slice(h * HEAD_DIM, (h + 1) * HEAD_DIM)
            delta = jnp.sum(
                grad_att[:, span].astype(F32) * att[part, :, span].astype(F32),
                axis=1, keepdims=True,
            )
            deltas = jnp.where(lane == h, delta, deltas)
        dcol[part] = deltas
        drow[part] = jnp.transpose(deltas)[:8]
        blocks.send(drow.at[part], twindow(part), es.at[part], er.at[part])
        gres_ref[part] = full2[part, group.me].astype(F32)
        query_side(part)
        if part < HALVES - 1:
            key_side(part)

    for h in range(HALVES):
        part = slice(h * rows, (h + 1) * rows)
        for cg in range(groups):
            span = slice(cg * width, (cg + 1) * width)
            second(2, h, cg).wait_recv()
            enc_ref[part, span] = unit[h, cg] * gain[:, span] + total(2, h, cg)
    key_side(HALVES - 1)

    for h in range(heads):
        khalo[h].left()
        vhalo[h].left()
    for h in range(HALVES):
        blocks.left(q.at[h], qwindow(h), qs.at[h], qr.at[h])
        blocks.left(do.at[h], dwindow(h), ds_.at[h], dr.at[h])
        blocks.left(drow.at[h], twindow(h), es.at[h], er.at[h])

        @pl.loop(0, groups)
        def _(cg):
            for stage in range(3):
                first(stage, h, cg).wait_send()
                second(stage, h, cg).wait_send()
            for kind in range(3):
                spread(0, full1, h, cg, kind).wait_send()
                spread(1, full2, h, cg, kind).wait_send()
    blocks.left(stat, swindow, ts, tr)


def layer(count, groups, q, k, v, res, w, gain, up, down, cg, source, cot):
    tok, head_cols = q.shape
    model = res.shape[1]
    heads = head_cols // HEAD_DIM
    src = up.shape[1]
    own = tok // groups
    rows, half, width = own // HALVES, tok // HALVES, model // groups
    copies = source.shape[1]
    dma = pltpu.SemaphoreType.DMA
    vm = pl.BlockSpec(memory_space=VM)
    far = pl.BlockSpec(memory_space=pl.ANY)
    grad = jax.ShapeDtypeStruct((tok, head_cols), F32)
    scratch = [
        VM(w.shape, BF16), VM(up.shape, BF16), VM(down.shape, BF16), VM((src, copies), BF16),
        VM((HALVES, half, model), BF16), VM((own, model), BF16),
        VM((1, model), F32), VM((1, copies), F32), VM((1, copies), jnp.int32),
        VM((heads, 5, tok, HEAD_DIM), BF16), VM((heads, 5, tok, HEAD_DIM), BF16),
        VM((HALVES, half, head_cols), BF16), VM((HALVES, 4, half, head_cols), BF16),
        VM((HALVES, half, head_cols), BF16), VM((HALVES, 4, half, head_cols), BF16),
        VM((heads, HALVES, half, 5 * tok), BF16), VM((heads, HALVES, tok, 4 * half), BF16),
        VM((HALVES, half, head_cols), BF16),
        VM((2 * heads, tok), F32), VM((4, 2 * heads, tok), F32),
        VM((HALVES, half, HEAD_DIM), F32), VM((HALVES, 8, half), F32), VM((HALVES, 4, 8, half), F32),
        VM((HALVES, half, src), F32), VM((HALVES, half, copies), F32), VM((HALVES, half, src), F32),
        VM((HALVES, half, copies), BF16), VM((half, copies), BF16),
        VM((HALVES, half, src), BF16), VM((HALVES, half, src), BF16), VM((half, head_cols), F32),
        VM((8, src), F32),
        VM((HALVES, groups, rows, width), F32), VM((HALVES, rows, HEAD_DIM), F32),
        VM((HALVES, groups, half, width), BF16), VM((HALVES, groups, half, width), BF16),
        VM((3, HALVES, groups, 2 * rows, width), BF16),
        VM((3, HALVES, groups, 2 * rows, width), BF16),
        VM((3, HALVES, groups, 2 * rows, width), BF16),
        VM((3, HALVES, groups, rows, width), BF16),
        VM((3, HALVES, groups, rows, width), BF16),
        dma((2 * heads + 6 + PIECES,)), dma((2, groups * HALVES)),
        dma((heads, 4)), dma((heads, 4)), dma((heads,)),
        dma((heads, 4)), dma((heads, 4)), dma((heads,)),
        dma((HALVES, 4)), dma((HALVES, 4)), dma((4,)), dma((4,)),
        dma((HALVES, 4)), dma((HALVES, 4)), dma((HALVES, 4)), dma((HALVES, 4)),
        dma((3, HALVES, groups)), dma((3, HALVES, groups)),
        dma((3, HALVES, groups)), dma((3, HALVES, groups)),
        dma((2, HALVES, groups, 3)), dma((2, HALVES, groups, 3)),
    ]
    return pl.pallas_call(
        functools.partial(layer_kernel, count),
        out_shape=(
            jax.ShapeDtypeStruct((own, model), F32),
            jax.ShapeDtypeStruct((HALVES, half, head_cols), F32),
            grad,
            grad,
            jax.ShapeDtypeStruct((HALVES, half, width), F32),
        ),
        in_specs=[far] * 11,
        out_specs=(vm,) * 5,
        scratch_shapes=scratch,
        compiler_params=pltpu.CompilerParams(
            collective_id=1, has_side_effects=True, vmem_limit_bytes=67043328
        ),
        name="layer",
    )(q, k, v, res, w, gain, up, down, cg, source, cot)


def emit_kernel(groups, enc, gq, gk, gv, gres, enc_out, gq_out, gk_out, gv_out, gres_out, sem):
    halves, half = gq.shape[:2]
    rows = half // groups
    own = halves * rows
    copies = [
        pltpu.make_async_copy(enc, enc_out, sem.at[0]),
        pltpu.make_async_copy(gk, gk_out, sem.at[1]),
        pltpu.make_async_copy(gv, gv_out, sem.at[2]),
    ]
    for i in range(groups * halves):
        owner, h = divmod(i, halves)
        there = pl.ds(owner * own + h * rows, rows)
        here = pl.ds(owner * rows, rows)
        copies.append(
            pltpu.make_async_copy(gq.at[h, here], gq_out.at[there], sem.at[3 + 2 * i])
        )
        copies.append(
            pltpu.make_async_copy(gres.at[h, here], gres_out.at[there], sem.at[4 + 2 * i])
        )
    for copy in copies:
        copy.start()
    for copy in copies:
        copy.wait()


def emit(groups, enc, gq, gk, gv, gres):
    halves, half, head_cols = gq.shape
    tok = halves * half
    grad = jax.ShapeDtypeStruct((tok, head_cols), F32)
    return pl.pallas_call(
        functools.partial(emit_kernel, groups),
        out_shape=(
            jax.ShapeDtypeStruct(enc.shape, F32), grad, grad, grad,
            jax.ShapeDtypeStruct((tok, gres.shape[2]), F32),
        ),
        in_specs=[pl.BlockSpec(memory_space=VM)] * 5,
        out_specs=(pl.BlockSpec(memory_space=pl.ANY),) * 5,
        scratch_shapes=[pltpu.SemaphoreType.DMA((3 + 2 * groups * halves,))],
        name="emit",
    )(enc, gq, gk, gv, gres)


def shards(
    count, groups, query_heads, key_heads, value_heads, residual, out_weight, ln_gain,
    up_source, down_source, copy_gain, neuron_source, cotangent,
):
    enc, gq, gk, gv, gres = layer(
        count, groups, query_heads, key_heads, value_heads, residual, out_weight,
        ln_gain[None, :], up_source, down_source, copy_gain[None, :], neuron_source[None, :],
        cotangent,
    )
    return emit(groups, enc, gq, gk, gv, gres)


def solution(mesh):
    in_specs = (
        P("seq", "tp"),
        P("seq", "tp"),
        P("seq", "tp"),
        P("seq", None),
        P("tp", None),
        P(),
        P(None, "tp"),
        P("tp", None),
        P("tp"),
        P("tp"),
        P("seq", None),
    )
    out_specs = (
        P(("seq", "tp"), None),
        P("seq", "tp"),
        P("seq", "tp"),
        P("seq", "tp"),
        P("seq", "tp"),
    )
    body = functools.partial(shards, mesh.shape["seq"], mesh.shape["tp"])
    return jax.shard_map(body, mesh=mesh, in_specs=in_specs, out_specs=out_specs, check_vma=False)
```

```python
import functools
import math

import jax
import jax.numpy as jnp
from jax import lax
from jax.experimental import pallas as pl
from jax.experimental.pallas import tpu as pltpu
from jax.sharding import PartitionSpec as P

HEAD_DIM = 128
OFFSETS = (-2, -1, 1, 2)
OWN = 4
HALVES = 2
PIECES = 4
TILE = 512
epsilon = 1e-05
MESH = pl.DeviceIdType.MESH
VM = pltpu.VMEM
F32 = jnp.float32
BF16 = jnp.bfloat16
SCALE = 1.0 / math.sqrt(HEAD_DIM)


def dot_nn(a, b):
    return jnp.dot(a, b, preferred_element_type=F32)


def dot_nt(a, b):
    return lax.dot_general(a, b, (((1,), (1,)), ((), ())), preferred_element_type=F32)


def dot_tn(a, b):
    return lax.dot_general(a, b, (((0,), (0,)), ((), ())), preferred_element_type=F32)


def remote(src, dst, send, recv, **where):
    return pltpu.make_async_remote_copy(
        src_ref=src, dst_ref=dst, send_sem=send, recv_sem=recv, device_id=where, device_id_type=MESH
    )


def gelu_slope(v):
    rate = math.sqrt(2.0 / math.pi)
    square = v * v
    bend = jnp.tanh(rate * v * (1.0 + 0.044715 * square))
    level = 0.5 * (1.0 + bend)
    slope = level + (0.5 * rate) * v * (1.0 - bend * bend) * (1.0 + 0.134145 * square)
    return v * level, slope


class Blocks:
    def __init__(self, count):
        self.count = count
        self.place = lax.axis_index("seq")
        self.even = lax.rem(self.place, 2) == 0

    def there(self, offset):
        other = self.place + offset
        return (other >= 0) & (other < self.count)

    def greet(self, barrier):
        for offset in OFFSETS:
            @pl.when(self.there(offset))
            def _():
                pl.semaphore_signal(
                    barrier, inc=1, device_id={"seq": self.place + offset}, device_id_type=MESH
                )

    def greeted(self, barrier, more):
        peers = sum(self.there(offset).astype(jnp.int32) for offset in OFFSETS)
        pl.semaphore_wait(barrier, peers + more)

    def copy(self, src, window, send, recv, index, slot):
        return remote(
            src, window(slot), send.at[index], recv.at[slot], seq=self.place + OFFSETS[index]
        )

    def send(self, src, window, send, recv):
        for index, offset in enumerate(OFFSETS):
            @pl.when(self.there(offset))
            def _():
                self.copy(src, window, send, recv, index, 3 - index).start()

    def arrive(self, src, window, send, recv):
        for index, offset in enumerate(OFFSETS):
            @pl.when(self.there(offset))
            def _():
                self.copy(src, window, send, recv, index, index).wait_recv()

    def left(self, src, window, send, recv):
        for index, offset in enumerate(OFFSETS):
            @pl.when(self.there(offset))
            def _():
                self.copy(src, window, send, recv, index, 3 - index).wait_send()

    def clear(self, window):
        for index, offset in enumerate(OFFSETS):
            @pl.when(jnp.logical_not(self.there(offset)))
            def _():
                ref = window(index)
                ref[...] = jnp.zeros(ref.shape, ref.dtype)


class Halo:
    def __init__(self, blocks, buf, send, recv, fwd, across):
        self.blocks, self.buf, self.send_sem, self.recv_sem, self.fwd = blocks, buf, send, recv, fwd
        self.across = across

    def window(self, slot):
        return self.buf.at[slot]

    def hops(self, even):
        return (0, 2 if even else 1, 3)

    def both(self, act):
        for even in (True, False):
            @pl.when(self.blocks.even == even)
            def _():
                act(even)

    def copy(self, index, slot):
        return self.blocks.copy(
            self.buf.at[OWN], self.window, self.send_sem, self.recv_sem, index, slot
        )

    def start(self):
        def act(even):
            for index in self.hops(even):
                @pl.when(self.blocks.there(OFFSETS[index]))
                def _():
                    self.copy(index, 3 - index).start()

        self.both(act)

    def passing(self, even):
        if self.across:
            return (3, 1, 2, 2) if even else (0, -1, 1, -2)
        return (2, 2, 1, 2) if even else (1, -2, 2, -2)

    def pass_copy(self, even):
        slot, to, there, need = self.passing(even)
        return remote(
            self.buf.at[slot], self.buf.at[there], self.fwd, self.recv_sem.at[there],
            seq=self.blocks.place + to,
        ), need

    def relay(self):
        def act(even):
            slot = self.passing(even)[0]
            copy, need = self.pass_copy(even)

            @pl.when(self.blocks.there(OFFSETS[slot]))
            def _():
                self.copy(slot, slot).wait_recv()

            @pl.when(self.blocks.there(need))
            def _():
                copy.start()

        self.both(act)

    def arrive(self):
        def act(even):
            for index in range(4):
                if index != self.passing(even)[0]:
                    @pl.when(self.blocks.there(OFFSETS[index]))
                    def _():
                        self.copy(index, index).wait_recv()

        self.both(act)

    def left(self):
        def act(even):
            for index in self.hops(even):
                @pl.when(self.blocks.there(OFFSETS[index]))
                def _():
                    self.copy(index, 3 - index).wait_send()
            copy, need = self.pass_copy(even)

            @pl.when(self.blocks.there(need))
            def _():
                copy.wait_send()

        self.both(act)


class Group:
    def __init__(self):
        me = lax.axis_index("tp")
        chip, core = lax.div(me, 2), lax.rem(me, 2)
        self.me = me
        self.sibling = chip * 2 + 1 - core
        self.far = (1 - chip) * 2 + core
        self.across = (1 - chip) * 2 + 1 - core

    def greet(self, barrier):
        for other in (self.sibling, self.far):
            pl.semaphore_signal(barrier, inc=1, device_id={"tp": other}, device_id_type=MESH)


def layer_kernel(
    count,
    q_hbm, k_hbm, v_hbm, res_hbm, w_hbm, gain_hbm, up_hbm, down_hbm, cg_hbm, src_hbm, cot_hbm,
    enc_ref, gq_ref, gk_ref, gv_ref, gres_ref, vown, qlast, dlast, tlast, plast,
    w, up, down, pick, cot, res, gain, cg_row, src_row,
    kbuf, vbuf, q, qwin, do, dwin, prob, probt, att, stat, swin, dcol, drow, twin,
    scaled, gcp, hid, actc, gcb, gh, gacc, inv, unit, sigma, full,
    sb, rb, mine, s2b, r2b,
    load_sem, slab_sem, cot_sem, ks, kr, kf, vs, vr, vf, qs, qr, ts, tr, ds_, dr, es, er,
    s1, r1, s2, r2, ags, agr,
):
    blocks, group = Blocks(count), Group()
    groups, rows, width = sb.shape[2], s2b.shape[3], s2b.shape[4]
    half = groups * rows
    own = HALVES * rows
    heads = kbuf.shape[0]
    tok = HALVES * half
    src = up.shape[1]
    depth = src // PIECES

    def cols(cg):
        return pl.ds(pl.multiple_of(cg * width, width), width)

    def slab(owner):
        return pl.ds(pl.multiple_of(owner * rows, rows), rows)

    loads = {}

    def load(name, source, target, sem):
        loads.setdefault(name, []).append(pltpu.make_async_copy(source, target, sem))

    def arrived(name):
        for copy in loads[name]:
            copy.wait()

    for h in range(heads):
        span = pl.ds(h * HEAD_DIM, HEAD_DIM)
        load("k", k_hbm.at[:, span], kbuf.at[h, OWN], load_sem.at[2 * h])
        load("v", v_hbm.at[:, span], vbuf.at[h, OWN], load_sem.at[2 * h + 1])
    at = 2 * heads
    load("src", src_hbm, src_row, load_sem.at[at])
    load("cg", cg_hbm, cg_row, load_sem.at[at + 1])
    load("gain", gain_hbm, gain, load_sem.at[at + 2])
    load("w", w_hbm, w, load_sem.at[at + 3])
    load("up", up_hbm, up, load_sem.at[at + 4])
    load("res", res_hbm.at[pl.ds(pl.multiple_of(group.me * own, own), own)], res, load_sem.at[at + 5])
    load("mine", cot_hbm.at[pl.ds(pl.multiple_of(group.me * own, own), own)], cot, load_sem.at[at + 6])
    at = at + 7
    for i in range(PIECES):
        span = pl.ds(i * depth, depth)
        load("down%d" % i, down_hbm.at[span], down.at[span], load_sem.at[at + i])
    for i in range(groups * HALVES):
        owner, h = divmod(i, HALVES)
        source = pl.ds(owner * own + h * rows, rows)
        for cg in range(groups):
            load(
                "cot", cot_hbm.at[source, pl.ds(cg * width, width)],
                full.at[h, cg, pl.ds(owner * rows, rows)], cot_sem.at[cg, i],
            )
        load("q", q_hbm.at[source], q.at[h, pl.ds(owner * rows, rows)], slab_sem.at[i])
    order = ["k", "v", "src", "cg", "q", "cot"] + ["down%d" % i for i in range(PIECES)]
    for name in order + ["gain", "w", "res", "mine", "up"]:
        for copy in loads[name]:
            copy.start()

    barrier = pltpu.get_barrier_semaphore()
    group.greet(barrier)
    blocks.greet(barrier)
    khalo = [Halo(blocks, kbuf.at[h], ks.at[h], kr.at[h], kf.at[h], True) for h in range(heads)]
    vhalo = [Halo(blocks, vbuf.at[h], vs.at[h], vr.at[h], vf.at[h], False) for h in range(heads)]
    arrived("k")
    arrived("v")
    blocks.greeted(barrier, 2)
    for h in range(heads):
        khalo[h].start()
        vhalo[h].start()

    last = HALVES - 1

    def qwindow(h):
        return lambda slot: qlast.at[slot] if h == last else qwin.at[h, slot]

    def dwindow(h):
        return lambda slot: dlast.at[slot] if h == last else dwin.at[h, slot]

    def twindow(h):
        return lambda slot: tlast.at[slot] if h == last else twin.at[h, slot]

    def swindow(slot):
        return swin.at[slot]

    def kslots(index):
        return kbuf.at[:, index]

    def vslots(index):
        return vbuf.at[:, index]

    blocks.clear(kslots)
    blocks.clear(vslots)
    for h in range(HALVES):
        blocks.clear(qwindow(h))
        blocks.clear(dwindow(h))
        blocks.clear(twindow(h))
    blocks.clear(lambda index: swin.at[index])

    arrived("src")
    arrived("cg")
    local = src_row[...] - group.me * src

    @pl.loop(0, PIECES)
    def _(i):
        place = lax.broadcasted_iota(jnp.int32, (depth, local.shape[1]), 0) + i * depth
        pick[pl.ds(pl.multiple_of(i * depth, depth), depth), :] = (
            jnp.where(place == local, 1.0, 0.0).astype(BF16)
        )

    ones = jnp.ones((16, local.shape[1]), BF16)
    inv[...] = 1.0 / (1.0 + dot_nt(ones, pick[...])[:8])

    def merged_grad(i):
        arrived("down%d" % i)
        span = slice(i * depth, (i + 1) * depth)
        part = jnp.zeros((tok, depth), F32)
        for cg in range(groups):
            part = part + dot_nt(
                full[:, cg].reshape(tok, width), down[span, cg * width : (cg + 1) * width]
            )
        part = part * inv[:1, span]
        scaled[:, :, span] = part.astype(BF16).reshape(HALVES, half, depth)

    stat_lane = lax.broadcasted_iota(jnp.int32, (tok, HEAD_DIM), 1)
    bias = jnp.concatenate(
        [
            jnp.full((1, tok), jnp.where(blocks.there(offset), 0.0, -1e30).astype(F32))
            for offset in OFFSETS
        ]
        + [jnp.zeros((1, tok), F32)],
        axis=1,
    )

    def attend(h, stats):
        khalo[h].arrive()
        vhalo[h].arrive()
        span = slice(h * HEAD_DIM, (h + 1) * HEAD_DIM)
        keys = kbuf[h].reshape(5 * tok, HEAD_DIM)
        scores = dot_nt(q[:, :, span].reshape(tok, HEAD_DIM), keys) * SCALE + bias
        top = jnp.max(scores, axis=1, keepdims=True)
        exps = jnp.exp(scores - top)
        inverse = 1.0 / jnp.sum(exps, axis=1, keepdims=True)
        low = (exps * inverse).astype(BF16)
        prob[h] = low.reshape(HALVES, half, 5 * tok)
        out = dot_nn(low, vbuf[h].reshape(5 * tok, HEAD_DIM)).astype(BF16)
        att[:, :, span] = out.reshape(HALVES, half, HEAD_DIM)
        stats = jnp.where(stat_lane == h, top, stats)
        return jnp.where(stat_lane == heads + h, inverse, stats)

    def relay(h):
        khalo[h].relay()
        vhalo[h].relay()

    stats = jnp.zeros((tok, HEAD_DIM), F32)
    relay(0)
    arrived("cot")
    merged_grad(0)
    relay(1)
    merged_grad(1)
    arrived("q")
    stats = attend(0, stats)
    relay(2)
    merged_grad(2)
    merged_grad(3)
    stats = attend(1, stats)
    relay(3)
    flat = scaled[...].reshape(tok, src)
    gcp[...] = (dot_nn(flat, pick[...]) * cg_row[...]).astype(BF16).reshape(gcp.shape)
    vown[...] = vbuf[:, OWN]
    for h in range(2, heads):
        stats = attend(h, stats)
    stat[...] = jnp.transpose(stats)[: 2 * heads]

    def first(stage, h, cg):
        return remote(
            sb.at[stage % 2, h, cg], rb.at[stage % 2, h, cg], s1.at[stage, h, cg], r1.at[stage, h, cg],
            tp=group.sibling,
        )

    def second(stage, h, cg):
        return remote(
            s2b.at[stage % 2, h, cg], r2b.at[stage % 2, h, cg], s2.at[stage, h, cg], r2.at[stage, h, cg],
            tp=group.far,
        )

    def hop1(stage, h, cg, lhs_ref, product):
        lhs = jnp.concatenate(
            [
                lhs_ref[h, slab(o), :]
                for o in (group.across, group.sibling, group.far, group.me)
            ],
            axis=0,
        )
        part = product(lhs, cg).astype(BF16)
        sb[stage % 2, h, cg] = part[: 2 * rows]
        mine[stage % 2, h, cg] = part[2 * rows :]
        first(stage, h, cg).start()

    def hop2(stage, h, cg):
        first(stage, h, cg).wait_recv()
        s2b[stage % 2, h, cg] = (
            mine[stage % 2, h, cg, :rows].astype(F32) + rb[stage % 2, h, cg, :rows].astype(F32)
        ).astype(BF16)
        second(stage, h, cg).start()

    def total(stage, h, cg):
        return (
            mine[stage % 2, h, cg, rows:].astype(F32)
            + rb[stage % 2, h, cg, rows:].astype(F32)
            + r2b[stage % 2, h, cg].astype(F32)
        )

    def spread(stage, full, h, cg, kind):
        owner = group.far if kind == 2 else group.me
        to = group.far if kind == 0 else group.sibling
        ref = full.at[h, cg, slab(owner)]
        return remote(ref, ref, ags.at[stage, h, cg, kind], agr.at[stage, h, cg, kind], tp=to)

    def spread_own(stage, full, h):
        for cg in range(groups):
            spread(stage, full, h, cg, 0).start()
            spread(stage, full, h, cg, 1).start()

    def pass_on(stage, full, h, cg):
        spread(stage, full, h, cg, 0).wait_recv()
        spread(stage, full, h, cg, 2).start()

    def gather(stage, full, h, use):
        pass_on(stage, full, h, 0)

        @pl.loop(0, groups)
        def _(cg):
            @pl.when(cg + 1 < groups)
            def _():
                pass_on(stage, full, h, cg + 1)

            spread(stage, full, h, cg, 1).wait_recv()
            spread(stage, full, h, cg, 2).wait_recv()
            use(cg)

    def out_product(lhs, cg):
        return dot_nn(lhs, w[:, cols(cg)])

    def back_product(lhs, cg):
        return dot_nt(lhs, up[cols(cg), :])

    def ffn_product(lhs, cg):
        return dot_nn(lhs, down[:, cols(cg)])

    def reduce_all(stage, lhs_ref, product):
        for h in range(HALVES):
            @pl.loop(0, groups)
            def _(cg):
                hop1(stage, h, cg, lhs_ref, product)
                if h > 0:
                    hop2(stage, h - 1, cg)

        @pl.loop(0, groups)
        def _(cg):
            hop2(stage, HALVES - 1, cg)

    arrived("w")
    reduce_all(0, att, out_product)
    for h in range(HALVES):
        blocks.send(q.at[h], qwindow(h), qs.at[h], qr.at[h])
    blocks.send(stat, swindow, ts, tr)

    arrived("res")
    arrived("gain")
    scale = 1.0 / (groups * width)
    for h in range(HALVES):
        part = slice(h * rows, (h + 1) * rows)
        sums = jnp.zeros((rows, 1), F32)
        for cg in range(groups):
            second(0, h, cg).wait_recv()
            stream = res[part, cg * width : (cg + 1) * width].astype(F32) + total(0, h, cg)
            unit[h, cg] = stream
            sums = sums + jnp.sum(stream, axis=1, keepdims=True)
        mean = sums * scale
        squares = jnp.zeros((rows, 1), F32)
        for cg in range(groups):
            centered = unit[h, cg] - mean
            squares = squares + jnp.sum(centered * centered, axis=1, keepdims=True)
        deviation = jnp.sqrt(squares * scale + epsilon)
        sigma[h] = jnp.broadcast_to(deviation, (rows, HEAD_DIM))
        for cg in range(groups):
            level = (unit[h, cg] - mean) / deviation
            unit[h, cg] = level
            full[h, cg, slab(group.me), :] = (
                level * gain[:, cg * width : (cg + 1) * width]
            ).astype(BF16)
        spread_own(0, full, h)

    arrived("up")
    tiles = src // TILE
    for h in range(HALVES):
        hid[h] = jnp.zeros(hid.shape[1:], F32)

        def use_hidden(cg):
            hid[h] += dot_nn(full[h, cg], up[cols(cg), :])

        gather(0, full, h, use_hidden)

        @pl.loop(0, tiles)
        def _(t):
            span = pl.ds(pl.multiple_of(t * TILE, TILE), TILE)
            copies = dot_nn(hid[h].astype(BF16), pick[:, span]) * cg_row[:, span]
            act, slope = gelu_slope(copies)
            actc[h, :, span] = act.astype(BF16)
            gcb[:, span] = (gcp[h, :, span].astype(F32) * slope).astype(BF16)

        @pl.loop(0, tiles)
        def _(t):
            span = pl.ds(pl.multiple_of(t * TILE, TILE), TILE)
            act, slope = gelu_slope(hid[h, :, span])
            hid[h, :, span] = act
            gh[h, :, span] = (
                scaled[h, :, span].astype(F32) * slope + dot_nt(gcb[...], pick[span, :])
            ).astype(BF16)

        @pl.loop(0, groups)
        def _(cg):
            for kind in range(3):
                spread(0, full, h, cg, kind).wait_send()
            hop1(1, h, cg, gh, back_product)

        @pl.loop(0, groups)
        def _(cg):
            hop2(1, h, cg)

    def feed_forward():
        @pl.loop(0, tiles)
        def _(t):
            span = pl.ds(pl.multiple_of(t * TILE, TILE), TILE)
            acts = hid[:, :, span].reshape(tok, TILE)
            copied = dot_nt(actc[...].reshape(tok, actc.shape[2]), pick[span, :])
            gh[:, :, span] = (
                ((acts + copied) * inv[:1, span]).astype(BF16).reshape(HALVES, half, TILE)
            )

        for h in range(HALVES):
            @pl.loop(0, groups)
            def _(cg):
                first(0, h, cg).wait_send()
                second(0, h, cg).wait_send()

        owners = (group.across, group.sibling, group.far, group.me)

        @pl.loop(0, groups)
        def _(cg):
            lhs = jnp.concatenate(
                [gh[h, slab(o), :] for h in range(HALVES) for o in owners], axis=0
            )
            part = ffn_product(lhs, cg).astype(BF16)
            for h in range(HALVES):
                sb[0, h, cg] = part[h * half : h * half + 2 * rows]
                mine[0, h, cg] = part[h * half + 2 * rows : (h + 1) * half]
                first(2, h, cg).start()

    arrived("mine")
    for h in range(HALVES):
        sums = jnp.zeros((rows, 1), F32)
        along = jnp.zeros((rows, 1), F32)
        pieces = []
        for cg in range(groups):
            span = slice(cg * width, (cg + 1) * width)
            second(1, h, cg).wait_recv()
            grad = cot[h * rows : (h + 1) * rows, span].astype(F32) + total(1, h, cg)
            graded = grad * gain[:, span]
            pieces.append(graded)
            sums = sums + jnp.sum(graded, axis=1, keepdims=True)
            along = along + jnp.sum(graded * unit[h, cg], axis=1, keepdims=True)
        for cg in range(groups):
            full[h, cg, slab(group.me), :] = (
                (pieces[cg] - sums * scale - unit[h, cg] * (along * scale)) / sigma[h, :, :1]
            ).astype(BF16)
        spread_own(1, full, h)
        if h == 0:
            feed_forward()

    for h in range(HALVES):
        @pl.loop(0, groups)
        def _(cg):
            hop2(2, h, cg)

    blocks.arrive(stat, swindow, ts, tr)
    for h in range(HALVES):
        blocks.arrive(q.at[h], qwindow(h), qs.at[h], qr.at[h])

    for part in range(HALVES):
        for h in range(heads):
            span = slice(h * HEAD_DIM, (h + 1) * HEAD_DIM)
            window = qlast if part == last else qwin.at[part]
            queries = window[:, :, span].reshape(4 * half, HEAD_DIM)
            lanes = slice(part * half, (part + 1) * half)
            top = jnp.concatenate([swin[s, h : h + 1, lanes] for s in range(4)], axis=1)
            inverse = jnp.concatenate(
                [swin[s, heads + h : heads + h + 1, lanes] for s in range(4)], axis=1
            )
            chance = jnp.exp(dot_nt(kbuf[h, OWN], queries) * SCALE - top) * inverse
            if part == last:
                plast[h] = chance.astype(BF16)
            else:
                probt[h, part] = chance.astype(BF16)

    lane = lax.broadcasted_iota(jnp.int32, (half, HEAD_DIM), 1)

    def query_side(part):
        for h in range(heads):
            span = slice(h * HEAD_DIM, (h + 1) * HEAD_DIM)
            grads = do[part, :, span]
            chance = prob[h, part]
            slope = (
                chance.astype(F32)
                * (
                    dot_nt(grads, vbuf[h].reshape(5 * tok, HEAD_DIM))
                    - dcol[part, :, h : h + 1]
                )
            ).astype(BF16)
            gq_ref[part, :, span] = dot_nn(slope, kbuf[h].reshape(5 * tok, HEAD_DIM)) * SCALE
            near = slice(OWN * tok, (OWN + 1) * tok)
            grad_k = dot_tn(slope[:, near], q[part, :, span]) * SCALE
            grad_v = dot_tn(chance[:, near], grads)
            if part == 0:
                gk_ref[:, span] = grad_k
                gv_ref[:, span] = grad_v
            else:
                gk_ref[:, span] += grad_k
                gv_ref[:, span] += grad_v

    def grads_arrive(part):
        blocks.arrive(do.at[part], dwindow(part), ds_.at[part], dr.at[part])
        blocks.arrive(drow.at[part], twindow(part), es.at[part], er.at[part])

    def key_side(part):
        grads_arrive(part)
        for h in range(heads):
            span = slice(h * HEAD_DIM, (h + 1) * HEAD_DIM)
            queries = qwin[part, :, :, span].reshape(4 * half, HEAD_DIM)
            grads = dwin[part, :, :, span].reshape(4 * half, HEAD_DIM)
            delta = jnp.concatenate([twin[part, s, h : h + 1, :] for s in range(4)], axis=1)
            chance = probt[h, part]
            slope = (chance.astype(F32) * (dot_nt(vbuf[h, OWN], grads) - delta)).astype(BF16)
            gv_ref[:, span] += dot_nn(chance, grads)
            gk_ref[:, span] += dot_nn(slope, queries) * SCALE

    for part in range(HALVES):
        gacc[...] = jnp.zeros(gacc.shape, F32)

        def use_low(cg):
            gacc[...] += dot_nt(full[part, cg], w[:, cols(cg)])

        gather(1, full, part, use_low)
        grad_att = gacc[...].astype(BF16)
        do[part] = grad_att
        blocks.send(do.at[part], dwindow(part), ds_.at[part], dr.at[part])
        deltas = jnp.zeros((half, HEAD_DIM), F32)
        for h in range(heads):
            span = slice(h * HEAD_DIM, (h + 1) * HEAD_DIM)
            delta = jnp.sum(
                grad_att[:, span].astype(F32) * att[part, :, span].astype(F32),
                axis=1, keepdims=True,
            )
            deltas = jnp.where(lane == h, delta, deltas)
        dcol[part] = deltas
        drow[part] = jnp.transpose(deltas)[:8]
        blocks.send(drow.at[part], twindow(part), es.at[part], er.at[part])
        gres_ref[part] = full[part, group.me]
        query_side(part)

    for part in range(last):
        key_side(part)

    for h in range(HALVES):
        part = slice(h * rows, (h + 1) * rows)
        for cg in range(groups):
            span = slice(cg * width, (cg + 1) * width)
            second(2, h, cg).wait_recv()
            enc_ref[part, span] = unit[h, cg] * gain[:, span] + total(2, h, cg)
    grads_arrive(last)

    for h in range(heads):
        khalo[h].left()
        vhalo[h].left()
    for h in range(HALVES):
        blocks.left(q.at[h], qwindow(h), qs.at[h], qr.at[h])
        blocks.left(do.at[h], dwindow(h), ds_.at[h], dr.at[h])
        blocks.left(drow.at[h], twindow(h), es.at[h], er.at[h])

        @pl.loop(0, groups)
        def _(cg):
            for stage in range(1, 3):
                first(stage, h, cg).wait_send()
                second(stage, h, cg).wait_send()
            for kind in range(3):
                spread(1, full, h, cg, kind).wait_send()
    blocks.left(stat, swindow, ts, tr)


def layer(count, groups, q, k, v, res, w, gain, up, down, cg, source, cot):
    tok, head_cols = q.shape
    model = res.shape[1]
    heads = head_cols // HEAD_DIM
    src = up.shape[1]
    own = tok // groups
    rows, half, width = own // HALVES, tok // HALVES, model // groups
    copies = source.shape[1]
    dma = pltpu.SemaphoreType.DMA
    vm = pl.BlockSpec(memory_space=VM)
    far = pl.BlockSpec(memory_space=pltpu.HBM)
    grad = jax.ShapeDtypeStruct((tok, head_cols), F32)
    scratch = [
        VM(w.shape, BF16), VM(up.shape, BF16), VM(down.shape, BF16), VM((src, copies), BF16),
        VM((own, model), BF16), VM((own, model), BF16),
        VM((1, model), F32), VM((1, copies), F32), VM((1, copies), jnp.int32),
        VM((heads, 5, tok, HEAD_DIM), BF16), VM((heads, 5, tok, HEAD_DIM), BF16),
        VM((HALVES, half, head_cols), BF16), VM((HALVES - 1, 4, half, head_cols), BF16),
        VM((HALVES, half, head_cols), BF16), VM((HALVES - 1, 4, half, head_cols), BF16),
        VM((heads, HALVES, half, 5 * tok), BF16), VM((heads, HALVES - 1, tok, 4 * half), BF16),
        VM((HALVES, half, head_cols), BF16),
        VM((2 * heads, tok), F32), VM((4, 2 * heads, tok), F32),
        VM((HALVES, half, HEAD_DIM), F32), VM((HALVES, 8, half), F32), VM((HALVES - 1, 4, 8, half), F32),
        VM((HALVES, half, src), BF16), VM((HALVES, half, copies), BF16), VM((HALVES, half, src), F32),
        VM((HALVES, half, copies), BF16), VM((half, copies), BF16),
        VM((HALVES, half, src), BF16), VM((half, head_cols), F32),
        VM((8, src), F32),
        VM((HALVES, groups, rows, width), F32), VM((HALVES, rows, HEAD_DIM), F32),
        VM((HALVES, groups, half, width), BF16),
        VM((2, HALVES, groups, 2 * rows, width), BF16),
        VM((2, HALVES, groups, 2 * rows, width), BF16),
        VM((2, HALVES, groups, 2 * rows, width), BF16),
        VM((2, HALVES, groups, rows, width), BF16),
        VM((2, HALVES, groups, rows, width), BF16),
        dma((2 * heads + 7 + PIECES,)), dma((groups * HALVES,)), dma((groups, groups * HALVES)),
        dma((heads, 4)), dma((heads, 4)), dma((heads,)),
        dma((heads, 4)), dma((heads, 4)), dma((heads,)),
        dma((HALVES, 4)), dma((HALVES, 4)), dma((4,)), dma((4,)),
        dma((HALVES, 4)), dma((HALVES, 4)), dma((HALVES, 4)), dma((HALVES, 4)),
        dma((3, HALVES, groups)), dma((3, HALVES, groups)),
        dma((3, HALVES, groups)), dma((3, HALVES, groups)),
        dma((2, HALVES, groups, 3)), dma((2, HALVES, groups, 3)),
    ]
    return pl.pallas_call(
        functools.partial(layer_kernel, count),
        out_shape=(
            jax.ShapeDtypeStruct((own, model), F32),
            jax.ShapeDtypeStruct((HALVES, half, head_cols), F32),
            grad,
            grad,
            jax.ShapeDtypeStruct((HALVES, half, width), BF16),
            jax.ShapeDtypeStruct((heads, tok, HEAD_DIM), BF16),
            jax.ShapeDtypeStruct((4, half, head_cols), BF16),
            jax.ShapeDtypeStruct((4, half, head_cols), BF16),
            jax.ShapeDtypeStruct((4, 8, half), F32),
            jax.ShapeDtypeStruct((heads, tok, 4 * half), BF16),
        ),
        in_specs=[far] * 11,
        out_specs=(vm,) * 10,
        scratch_shapes=scratch,
        compiler_params=pltpu.CompilerParams(
            collective_id=1, has_side_effects=True, vmem_limit_bytes=50855936
        ),
        name="layer",
    )(*[
        pltpu.with_memory_space_constraint(x, pltpu.HBM)
        for x in (q, k, v, res, w, gain, up, down, cg, source, cot)
    ])


def emit_kernel(
    groups, enc, gq, gk, gv, gres, vown, qlast, dlast, tlast, plast,
    enc_out, gq_out, gk_out, gv_out, gres_out, gk_sum, gv_sum, wide, sem, head_sem,
):
    halves, half = gq.shape[:2]
    rows = half // groups
    own = halves * rows
    heads = vown.shape[0]
    copies = [pltpu.make_async_copy(enc, enc_out, sem.at[0])]
    copies[0].start()
    wide[...] = gres[...].astype(F32)
    for i in range(groups * halves):
        owner, h = divmod(i, halves)
        there = pl.ds(owner * own + h * rows, rows)
        here = pl.ds(owner * rows, rows)
        copies.append(
            pltpu.make_async_copy(gq.at[h, here], gq_out.at[there], sem.at[1 + 2 * i])
        )
        copies.append(
            pltpu.make_async_copy(wide.at[h, here], gres_out.at[there], sem.at[2 + 2 * i])
        )
    for copy in copies[1:]:
        copy.start()
    for h in range(heads):
        span = slice(h * HEAD_DIM, (h + 1) * HEAD_DIM)
        queries = qlast[:, :, span].reshape(4 * half, HEAD_DIM)
        grads = dlast[:, :, span].reshape(4 * half, HEAD_DIM)
        delta = jnp.concatenate([tlast[s, h : h + 1, :] for s in range(4)], axis=1)
        chance = plast[h]
        slope = (chance.astype(F32) * (dot_nt(vown[h], grads) - delta)).astype(BF16)
        gv_sum[h] = gv[:, span] + dot_nn(chance, grads)
        gk_sum[h] = gk[:, span] + dot_nn(slope, queries) * SCALE
        there = pl.ds(h * HEAD_DIM, HEAD_DIM)
        outs = [
            pltpu.make_async_copy(gv_sum.at[h], gv_out.at[:, there], head_sem.at[0, h]),
            pltpu.make_async_copy(gk_sum.at[h], gk_out.at[:, there], head_sem.at[1, h]),
        ]
        for copy in outs:
            copy.start()
        copies += outs
    for copy in copies:
        copy.wait()


def emit(groups, enc, gq, gk, gv, gres, vown, *rest):
    halves, half, head_cols = gq.shape
    tok = halves * half
    heads = vown.shape[0]
    grad = jax.ShapeDtypeStruct((tok, head_cols), F32)
    return pl.pallas_call(
        functools.partial(emit_kernel, groups),
        out_shape=(
            jax.ShapeDtypeStruct(enc.shape, F32), grad, grad, grad,
            jax.ShapeDtypeStruct((tok, gres.shape[2]), F32),
        ),
        in_specs=[pl.BlockSpec(memory_space=VM)] * 10,
        out_specs=(pl.BlockSpec(memory_space=pl.ANY),) * 5,
        scratch_shapes=[
            VM((heads, tok, HEAD_DIM), F32),
            VM((heads, tok, HEAD_DIM), F32),
            VM(gres.shape, F32),
            pltpu.SemaphoreType.DMA((1 + 2 * groups * halves,)),
            pltpu.SemaphoreType.DMA((2, heads)),
        ],
        compiler_params=pltpu.CompilerParams(vmem_limit_bytes=24 << 20),
        name="emit",
    )(enc, gq, gk, gv, gres, vown, *rest)


def shards(
    count, groups, query_heads, key_heads, value_heads, residual, out_weight, ln_gain,
    up_source, down_source, copy_gain, neuron_source, cotangent,
):
    parts = layer(
        count, groups, query_heads, key_heads, value_heads, residual, out_weight,
        ln_gain[None, :], up_source, down_source, copy_gain[None, :], neuron_source[None, :],
        cotangent,
    )
    return emit(groups, *parts)


def solution(mesh):
    in_specs = (
        P("seq", "tp"),
        P("seq", "tp"),
        P("seq", "tp"),
        P("seq", None),
        P("tp", None),
        P(),
        P(None, "tp"),
        P("tp", None),
        P("tp"),
        P("tp"),
        P("seq", None),
    )
    out_specs = (
        P(("seq", "tp"), None),
        P("seq", "tp"),
        P("seq", "tp"),
        P("seq", "tp"),
        P("seq", "tp"),
    )
    body = functools.partial(shards, mesh.shape["seq"], mesh.shape["tp"])
    return jax.shard_map(body, mesh=mesh, in_specs=in_specs, out_specs=out_specs, check_vma=False)
```

```python
import functools
import math

import jax
import jax.numpy as jnp
from jax import lax
from jax.experimental import pallas as pl
from jax.experimental.pallas import tpu as pltpu
from jax.sharding import PartitionSpec as P

HEAD_DIM = 128
OFFSETS = (-2, -1, 1, 2)
OWN = 4
HALVES = 2
PIECES = 4
TILE = 512
epsilon = 1e-05
MESH = pl.DeviceIdType.MESH
VM = pltpu.VMEM
F32 = jnp.float32
BF16 = jnp.bfloat16
SCALE = 1.0 / math.sqrt(HEAD_DIM)


def dot_nn(a, b):
    return jnp.dot(a, b, preferred_element_type=F32)


def dot_nt(a, b):
    return lax.dot_general(a, b, (((1,), (1,)), ((), ())), preferred_element_type=F32)


def dot_tn(a, b):
    return lax.dot_general(a, b, (((0,), (0,)), ((), ())), preferred_element_type=F32)


def remote(src, dst, send, recv, **where):
    return pltpu.make_async_remote_copy(
        src_ref=src, dst_ref=dst, send_sem=send, recv_sem=recv, device_id=where, device_id_type=MESH
    )


def gelu_slope(v):
    rate = math.sqrt(2.0 / math.pi)
    square = v * v
    bend = jnp.tanh(rate * v * (1.0 + 0.044715 * square))
    level = 0.5 * (1.0 + bend)
    slope = level + (0.5 * rate) * v * (1.0 - bend * bend) * (1.0 + 0.134145 * square)
    return v * level, slope


class Blocks:
    def __init__(self, count):
        self.count = count
        self.place = lax.axis_index("seq")
        self.even = lax.rem(self.place, 2) == 0

    def there(self, offset):
        other = self.place + offset
        return (other >= 0) & (other < self.count)

    def greet(self, barrier):
        for offset in OFFSETS:
            @pl.when(self.there(offset))
            def _():
                pl.semaphore_signal(
                    barrier, inc=1, device_id={"seq": self.place + offset}, device_id_type=MESH
                )

    def greeted(self, barrier, more):
        peers = sum(self.there(offset).astype(jnp.int32) for offset in OFFSETS)
        pl.semaphore_wait(barrier, peers + more)

    def copy(self, src, window, send, recv, index, slot):
        return remote(
            src, window(slot), send.at[index], recv.at[slot], seq=self.place + OFFSETS[index]
        )

    def send(self, src, window, send, recv):
        for index, offset in enumerate(OFFSETS):
            @pl.when(self.there(offset))
            def _():
                self.copy(src, window, send, recv, index, 3 - index).start()

    def arrive(self, src, window, send, recv):
        for index, offset in enumerate(OFFSETS):
            @pl.when(self.there(offset))
            def _():
                self.copy(src, window, send, recv, index, index).wait_recv()

    def left(self, src, window, send, recv):
        for index, offset in enumerate(OFFSETS):
            @pl.when(self.there(offset))
            def _():
                self.copy(src, window, send, recv, index, 3 - index).wait_send()

    def clear(self, window):
        for index, offset in enumerate(OFFSETS):
            @pl.when(jnp.logical_not(self.there(offset)))
            def _():
                ref = window(index)
                ref[...] = jnp.zeros(ref.shape, ref.dtype)


class Halo:
    def __init__(self, blocks, buf, send, recv, fwd, across):
        self.blocks, self.buf, self.send_sem, self.recv_sem, self.fwd = blocks, buf, send, recv, fwd
        self.across = across

    def window(self, slot):
        return self.buf.at[slot]

    def hops(self, even):
        return (0, 2 if even else 1, 3)

    def both(self, act):
        for even in (True, False):
            @pl.when(self.blocks.even == even)
            def _():
                act(even)

    def copy(self, index, slot):
        return self.blocks.copy(
            self.buf.at[OWN], self.window, self.send_sem, self.recv_sem, index, slot
        )

    def start(self):
        def act(even):
            for index in self.hops(even):
                @pl.when(self.blocks.there(OFFSETS[index]))
                def _():
                    self.copy(index, 3 - index).start()

        self.both(act)

    def passing(self, even):
        if self.across:
            return (3, 1, 2, 2) if even else (0, -1, 1, -2)
        return (2, 2, 1, 2) if even else (1, -2, 2, -2)

    def pass_copy(self, even):
        slot, to, there, need = self.passing(even)
        return remote(
            self.buf.at[slot], self.buf.at[there], self.fwd, self.recv_sem.at[there],
            seq=self.blocks.place + to,
        ), need

    def relay(self):
        def act(even):
            slot = self.passing(even)[0]
            copy, need = self.pass_copy(even)

            @pl.when(self.blocks.there(OFFSETS[slot]))
            def _():
                self.copy(slot, slot).wait_recv()

            @pl.when(self.blocks.there(need))
            def _():
                copy.start()

        self.both(act)

    def arrive(self):
        def act(even):
            for index in range(4):
                if index != self.passing(even)[0]:
                    @pl.when(self.blocks.there(OFFSETS[index]))
                    def _():
                        self.copy(index, index).wait_recv()

        self.both(act)

    def left(self):
        def act(even):
            for index in self.hops(even):
                @pl.when(self.blocks.there(OFFSETS[index]))
                def _():
                    self.copy(index, 3 - index).wait_send()
            copy, need = self.pass_copy(even)

            @pl.when(self.blocks.there(need))
            def _():
                copy.wait_send()

        self.both(act)


class Group:
    def __init__(self):
        me = lax.axis_index("tp")
        chip, core = lax.div(me, 2), lax.rem(me, 2)
        self.me = me
        self.sibling = chip * 2 + 1 - core
        self.far = (1 - chip) * 2 + core
        self.across = (1 - chip) * 2 + 1 - core

    def greet(self, barrier):
        for other in (self.sibling, self.far):
            pl.semaphore_signal(barrier, inc=1, device_id={"tp": other}, device_id_type=MESH)


def layer_kernel(
    count,
    q_hbm, k_hbm, v_hbm, res_hbm, w_hbm, gain_hbm, up_hbm, down_hbm, cg_hbm, src_hbm, cot_hbm,
    enc_ref, gq_ref, gk_ref, gv_ref, gres_ref, vown, qlast, dlast, tlast, plast,
    w, up, down, pick, cot, res, gain, cg_row, src_row,
    kbuf, vbuf, q, qwin, do, dwin, prob, probt, att, stat, swin, dcol, drow, twin,
    scaled, gcp, hid, actc, gcb, gh, gacc, inv, unit, sigma, full,
    sb, rb, mine, s2b, r2b,
    load_sem, slab_sem, cot_sem, ks, kr, kf, vs, vr, vf, qs, qr, ts, tr, ds_, dr, es, er,
    s1, r1, s2, r2, ags, agr,
):
    blocks, group = Blocks(count), Group()
    groups, rows, width = sb.shape[2], s2b.shape[3], s2b.shape[4]
    half = groups * rows
    own = HALVES * rows
    heads = kbuf.shape[0]
    tok = HALVES * half
    src = up.shape[1]
    depth = src // PIECES

    def cols(cg):
        return pl.ds(pl.multiple_of(cg * width, width), width)

    def slab(owner):
        return pl.ds(pl.multiple_of(owner * rows, rows), rows)

    loads = {}

    def load(name, source, target, sem):
        loads.setdefault(name, []).append(pltpu.make_async_copy(source, target, sem))

    def arrived(name):
        for copy in loads[name]:
            copy.wait()

    for h in range(heads):
        span = pl.ds(h * HEAD_DIM, HEAD_DIM)
        load("k", k_hbm.at[:, span], kbuf.at[h, OWN], load_sem.at[2 * h])
        load("v", v_hbm.at[:, span], vbuf.at[h, OWN], load_sem.at[2 * h + 1])
    at = 2 * heads
    load("src", src_hbm, src_row, load_sem.at[at])
    load("cg", cg_hbm, cg_row, load_sem.at[at + 1])
    load("gain", gain_hbm, gain, load_sem.at[at + 2])
    load("w", w_hbm, w, load_sem.at[at + 3])
    load("up", up_hbm, up, load_sem.at[at + 4])
    load("res", res_hbm.at[pl.ds(pl.multiple_of(group.me * own, own), own)], res, load_sem.at[at + 5])
    load("mine", cot_hbm.at[pl.ds(pl.multiple_of(group.me * own, own), own)], cot, load_sem.at[at + 6])
    at = at + 7
    for i in range(PIECES):
        span = pl.ds(i * depth, depth)
        load("down%d" % i, down_hbm.at[span], down.at[span], load_sem.at[at + i])
    for i in range(groups * HALVES):
        owner, h = divmod(i, HALVES)
        source = pl.ds(owner * own + h * rows, rows)
        for cg in range(groups):
            load(
                "cot", cot_hbm.at[source, pl.ds(cg * width, width)],
                full.at[h, cg, pl.ds(owner * rows, rows)], cot_sem.at[cg, i],
            )
        load("q", q_hbm.at[source], q.at[h, pl.ds(owner * rows, rows)], slab_sem.at[i])
    order = ["k", "v", "src", "cg", "q", "cot"] + ["down%d" % i for i in range(PIECES)]
    for name in order + ["gain", "w", "res", "mine", "up"]:
        for copy in loads[name]:
            copy.start()

    barrier = pltpu.get_barrier_semaphore()
    group.greet(barrier)
    blocks.greet(barrier)
    khalo = [Halo(blocks, kbuf.at[h], ks.at[h], kr.at[h], kf.at[h], True) for h in range(heads)]
    vhalo = [Halo(blocks, vbuf.at[h], vs.at[h], vr.at[h], vf.at[h], False) for h in range(heads)]
    arrived("k")
    arrived("v")
    blocks.greeted(barrier, 2)
    for h in range(heads):
        khalo[h].start()
        vhalo[h].start()

    last = HALVES - 1

    def qwindow(h):
        return lambda slot: qlast.at[slot] if h == last else qwin.at[h, slot]

    def dwindow(h):
        return lambda slot: dlast.at[slot] if h == last else dwin.at[h, slot]

    def twindow(h):
        return lambda slot: tlast.at[slot] if h == last else twin.at[h, slot]

    def swindow(slot):
        return swin.at[slot]

    def kslots(index):
        return kbuf.at[:, index]

    def vslots(index):
        return vbuf.at[:, index]

    blocks.clear(kslots)
    blocks.clear(vslots)
    for h in range(HALVES):
        blocks.clear(qwindow(h))
        blocks.clear(dwindow(h))
        blocks.clear(twindow(h))
    blocks.clear(lambda index: swin.at[index])

    arrived("src")
    arrived("cg")
    local = src_row[...] - group.me * src

    @pl.loop(0, PIECES)
    def _(i):
        place = lax.broadcasted_iota(jnp.int32, (depth, local.shape[1]), 0) + i * depth
        pick[pl.ds(pl.multiple_of(i * depth, depth), depth), :] = (
            jnp.where(place == local, 1.0, 0.0).astype(BF16)
        )

    ones = jnp.ones((16, local.shape[1]), BF16)
    inv[...] = 1.0 / (1.0 + dot_nt(ones, pick[...])[:8])

    def merged_grad(i):
        arrived("down%d" % i)
        span = slice(i * depth, (i + 1) * depth)
        part = jnp.zeros((tok, depth), F32)
        for cg in range(groups):
            part = part + dot_nt(
                full[:, cg].reshape(tok, width), down[span, cg * width : (cg + 1) * width]
            )
        part = part * inv[:1, span]
        scaled[:, :, span] = part.astype(BF16).reshape(HALVES, half, depth)

    stat_lane = lax.broadcasted_iota(jnp.int32, (tok, HEAD_DIM), 1)
    bias = jnp.concatenate(
        [
            jnp.full((1, tok), jnp.where(blocks.there(offset), 0.0, -1e30).astype(F32))
            for offset in OFFSETS
        ]
        + [jnp.zeros((1, tok), F32)],
        axis=1,
    )

    def attend(h, stats):
        khalo[h].arrive()
        vhalo[h].arrive()
        span = slice(h * HEAD_DIM, (h + 1) * HEAD_DIM)
        keys = kbuf[h].reshape(5 * tok, HEAD_DIM)
        scores = dot_nt(q[:, :, span].reshape(tok, HEAD_DIM), keys) * SCALE + bias
        top = jnp.max(scores, axis=1, keepdims=True)
        exps = jnp.exp(scores - top)
        inverse = 1.0 / jnp.sum(exps, axis=1, keepdims=True)
        low = (exps * inverse).astype(BF16)
        prob[h] = low.reshape(HALVES, half, 5 * tok)
        out = dot_nn(low, vbuf[h].reshape(5 * tok, HEAD_DIM)).astype(BF16)
        att[:, :, span] = out.reshape(HALVES, half, HEAD_DIM)
        stats = jnp.where(stat_lane == h, top, stats)
        return jnp.where(stat_lane == heads + h, inverse, stats)

    def relay(h):
        khalo[h].relay()
        vhalo[h].relay()

    stats = jnp.zeros((tok, HEAD_DIM), F32)
    relay(0)
    arrived("cot")
    merged_grad(0)
    relay(1)
    merged_grad(1)
    arrived("q")
    stats = attend(0, stats)
    relay(2)
    merged_grad(2)
    merged_grad(3)
    stats = attend(1, stats)
    relay(3)
    flat = scaled[...].reshape(tok, src)
    gcp[...] = (dot_nn(flat, pick[...]) * cg_row[...]).astype(BF16).reshape(gcp.shape)
    vown[...] = vbuf[:, OWN]
    for h in range(2, heads):
        stats = attend(h, stats)
    stat[...] = jnp.transpose(stats)[: 2 * heads]

    def first(stage, h, cg):
        return remote(
            sb.at[stage % 2, h, cg], rb.at[stage % 2, h, cg], s1.at[stage, h, cg], r1.at[stage, h, cg],
            tp=group.sibling,
        )

    def second(stage, h, cg):
        return remote(
            s2b.at[stage % 2, h, cg], r2b.at[stage % 2, h, cg], s2.at[stage, h, cg], r2.at[stage, h, cg],
            tp=group.far,
        )

    def hop1(stage, h, cg, lhs_ref, product):
        lhs = jnp.concatenate(
            [
                lhs_ref[h, slab(o), :]
                for o in (group.across, group.sibling, group.far, group.me)
            ],
            axis=0,
        )
        part = product(lhs, cg).astype(BF16)
        sb[stage % 2, h, cg] = part[: 2 * rows]
        mine[stage % 2, h, cg] = part[2 * rows :]
        first(stage, h, cg).start()

    def hop2(stage, h, cg):
        first(stage, h, cg).wait_recv()
        s2b[stage % 2, h, cg] = (
            mine[stage % 2, h, cg, :rows].astype(F32) + rb[stage % 2, h, cg, :rows].astype(F32)
        ).astype(BF16)
        second(stage, h, cg).start()

    def total(stage, h, cg):
        return (
            mine[stage % 2, h, cg, rows:].astype(F32)
            + rb[stage % 2, h, cg, rows:].astype(F32)
            + r2b[stage % 2, h, cg].astype(F32)
        )

    def spread(stage, full, h, cg, kind):
        owner = group.far if kind == 2 else group.me
        to = group.far if kind == 0 else group.sibling
        ref = full.at[h, cg, slab(owner)]
        return remote(ref, ref, ags.at[stage, h, cg, kind], agr.at[stage, h, cg, kind], tp=to)

    def spread_own(stage, full, h):
        for cg in range(groups):
            spread(stage, full, h, cg, 0).start()
            spread(stage, full, h, cg, 1).start()

    def pass_on(stage, full, h, cg):
        spread(stage, full, h, cg, 0).wait_recv()
        spread(stage, full, h, cg, 2).start()

    def gather(stage, full, h, use):
        pass_on(stage, full, h, 0)

        @pl.loop(0, groups)
        def _(cg):
            @pl.when(cg + 1 < groups)
            def _():
                pass_on(stage, full, h, cg + 1)

            spread(stage, full, h, cg, 1).wait_recv()
            spread(stage, full, h, cg, 2).wait_recv()
            use(cg)

    def out_product(lhs, cg):
        return dot_nn(lhs, w[:, cols(cg)])

    def back_product(lhs, cg):
        return dot_nt(lhs, up[cols(cg), :])

    def ffn_product(lhs, cg):
        return dot_nn(lhs, down[:, cols(cg)])

    def reduce_all(stage, lhs_ref, product):
        for h in range(HALVES):
            @pl.loop(0, groups)
            def _(cg):
                hop1(stage, h, cg, lhs_ref, product)
                if h > 0:
                    hop2(stage, h - 1, cg)

        @pl.loop(0, groups)
        def _(cg):
            hop2(stage, HALVES - 1, cg)

    arrived("w")
    reduce_all(0, att, out_product)
    for h in range(HALVES):
        blocks.send(q.at[h], qwindow(h), qs.at[h], qr.at[h])
    blocks.send(stat, swindow, ts, tr)

    arrived("res")
    arrived("gain")
    scale = 1.0 / (groups * width)
    for h in range(HALVES):
        part = slice(h * rows, (h + 1) * rows)
        sums = jnp.zeros((rows, 1), F32)
        for cg in range(groups):
            second(0, h, cg).wait_recv()
            stream = res[part, cg * width : (cg + 1) * width].astype(F32) + total(0, h, cg)
            unit[h, cg] = stream
            sums = sums + jnp.sum(stream, axis=1, keepdims=True)
        mean = sums * scale
        squares = jnp.zeros((rows, 1), F32)
        for cg in range(groups):
            centered = unit[h, cg] - mean
            squares = squares + jnp.sum(centered * centered, axis=1, keepdims=True)
        deviation = jnp.sqrt(squares * scale + epsilon)
        sigma[h] = jnp.broadcast_to(deviation, (rows, HEAD_DIM))
        for cg in range(groups):
            level = (unit[h, cg] - mean) / deviation
            unit[h, cg] = level
            full[h, cg, slab(group.me), :] = (
                level * gain[:, cg * width : (cg + 1) * width]
            ).astype(BF16)
        spread_own(0, full, h)

    arrived("up")
    tiles = src // TILE
    for h in range(HALVES):
        hid[h] = jnp.zeros(hid.shape[1:], F32)

        def use_hidden(cg):
            hid[h] += dot_nn(full[h, cg], up[cols(cg), :])

        gather(0, full, h, use_hidden)

        @pl.loop(0, tiles)
        def _(t):
            span = pl.ds(pl.multiple_of(t * TILE, TILE), TILE)
            copies = dot_nn(hid[h].astype(BF16), pick[:, span]) * cg_row[:, span]
            act, slope = gelu_slope(copies)
            actc[h, :, span] = act.astype(BF16)
            gcb[:, span] = (gcp[h, :, span].astype(F32) * slope).astype(BF16)

        @pl.loop(0, tiles)
        def _(t):
            span = pl.ds(pl.multiple_of(t * TILE, TILE), TILE)
            act, slope = gelu_slope(hid[h, :, span])
            hid[h, :, span] = act
            gh[h, :, span] = (
                scaled[h, :, span].astype(F32) * slope + dot_nt(gcb[...], pick[span, :])
            ).astype(BF16)

        @pl.loop(0, groups)
        def _(cg):
            for kind in range(3):
                spread(0, full, h, cg, kind).wait_send()
            hop1(1, h, cg, gh, back_product)

            @pl.when(cg > 0)
            def _():
                hop2(1, h, cg - 1)

        hop2(1, h, groups - 1)

    def feed_forward():
        @pl.loop(0, tiles)
        def _(t):
            span = pl.ds(pl.multiple_of(t * TILE, TILE), TILE)
            acts = hid[:, :, span].reshape(tok, TILE)
            copied = dot_nt(actc[...].reshape(tok, actc.shape[2]), pick[span, :])
            gh[:, :, span] = (
                ((acts + copied) * inv[:1, span]).astype(BF16).reshape(HALVES, half, TILE)
            )

        for h in range(HALVES):
            @pl.loop(0, groups)
            def _(cg):
                first(0, h, cg).wait_send()
                second(0, h, cg).wait_send()

        owners = (group.across, group.sibling, group.far, group.me)

        @pl.loop(0, groups)
        def _(cg):
            lhs = jnp.concatenate(
                [gh[h, slab(o), :] for h in range(HALVES) for o in owners], axis=0
            )
            part = ffn_product(lhs, cg).astype(BF16)
            for h in range(HALVES):
                sb[0, h, cg] = part[h * half : h * half + 2 * rows]
                mine[0, h, cg] = part[h * half + 2 * rows : (h + 1) * half]
                first(2, h, cg).start()

    arrived("mine")
    for h in range(HALVES):
        sums = jnp.zeros((rows, 1), F32)
        along = jnp.zeros((rows, 1), F32)
        pieces = []
        for cg in range(groups):
            span = slice(cg * width, (cg + 1) * width)
            second(1, h, cg).wait_recv()
            grad = cot[h * rows : (h + 1) * rows, span].astype(F32) + total(1, h, cg)
            graded = grad * gain[:, span]
            pieces.append(graded)
            sums = sums + jnp.sum(graded, axis=1, keepdims=True)
            along = along + jnp.sum(graded * unit[h, cg], axis=1, keepdims=True)
        for cg in range(groups):
            full[h, cg, slab(group.me), :] = (
                (pieces[cg] - sums * scale - unit[h, cg] * (along * scale)) / sigma[h, :, :1]
            ).astype(BF16)
        spread_own(1, full, h)
        if h == 0:
            feed_forward()

    for h in range(HALVES):
        @pl.loop(0, groups)
        def _(cg):
            hop2(2, h, cg)

    blocks.arrive(stat, swindow, ts, tr)
    for h in range(HALVES):
        blocks.arrive(q.at[h], qwindow(h), qs.at[h], qr.at[h])

    for part in range(HALVES):
        for h in range(heads):
            span = slice(h * HEAD_DIM, (h + 1) * HEAD_DIM)
            window = qlast if part == last else qwin.at[part]
            queries = window[:, :, span].reshape(4 * half, HEAD_DIM)
            lanes = slice(part * half, (part + 1) * half)
            top = jnp.concatenate([swin[s, h : h + 1, lanes] for s in range(4)], axis=1)
            inverse = jnp.concatenate(
                [swin[s, heads + h : heads + h + 1, lanes] for s in range(4)], axis=1
            )
            chance = jnp.exp(dot_nt(kbuf[h, OWN], queries) * SCALE - top) * inverse
            if part == last:
                plast[h] = chance.astype(BF16)
            else:
                probt[h, part] = chance.astype(BF16)

    lane = lax.broadcasted_iota(jnp.int32, (half, HEAD_DIM), 1)

    def query_side(part):
        for h in range(heads):
            span = slice(h * HEAD_DIM, (h + 1) * HEAD_DIM)
            grads = do[part, :, span]
            chance = prob[h, part]
            slope = (
                chance.astype(F32)
                * (
                    dot_nt(grads, vbuf[h].reshape(5 * tok, HEAD_DIM))
                    - dcol[part, :, h : h + 1]
                )
            ).astype(BF16)
            gq_ref[part, :, span] = dot_nn(slope, kbuf[h].reshape(5 * tok, HEAD_DIM)) * SCALE
            near = slice(OWN * tok, (OWN + 1) * tok)
            grad_k = dot_tn(slope[:, near], q[part, :, span]) * SCALE
            grad_v = dot_tn(chance[:, near], grads)
            if part == 0:
                gk_ref[:, span] = grad_k
                gv_ref[:, span] = grad_v
            else:
                gk_ref[:, span] += grad_k
                gv_ref[:, span] += grad_v

    def grads_arrive(part):
        blocks.arrive(do.at[part], dwindow(part), ds_.at[part], dr.at[part])
        blocks.arrive(drow.at[part], twindow(part), es.at[part], er.at[part])

    def key_side(part):
        grads_arrive(part)
        for h in range(heads):
            span = slice(h * HEAD_DIM, (h + 1) * HEAD_DIM)
            queries = qwin[part, :, :, span].reshape(4 * half, HEAD_DIM)
            grads = dwin[part, :, :, span].reshape(4 * half, HEAD_DIM)
            delta = jnp.concatenate([twin[part, s, h : h + 1, :] for s in range(4)], axis=1)
            chance = probt[h, part]
            slope = (chance.astype(F32) * (dot_nt(vbuf[h, OWN], grads) - delta)).astype(BF16)
            gv_ref[:, span] += dot_nn(chance, grads)
            gk_ref[:, span] += dot_nn(slope, queries) * SCALE

    for part in range(HALVES):
        gacc[...] = jnp.zeros(gacc.shape, F32)

        def use_low(cg):
            gacc[...] += dot_nt(full[part, cg], w[:, cols(cg)])

        gather(1, full, part, use_low)
        grad_att = gacc[...].astype(BF16)
        do[part] = grad_att
        blocks.send(do.at[part], dwindow(part), ds_.at[part], dr.at[part])
        deltas = jnp.zeros((half, HEAD_DIM), F32)
        for h in range(heads):
            span = slice(h * HEAD_DIM, (h + 1) * HEAD_DIM)
            delta = jnp.sum(
                grad_att[:, span].astype(F32) * att[part, :, span].astype(F32),
                axis=1, keepdims=True,
            )
            deltas = jnp.where(lane == h, delta, deltas)
        dcol[part] = deltas
        drow[part] = jnp.transpose(deltas)[:8]
        blocks.send(drow.at[part], twindow(part), es.at[part], er.at[part])
        gres_ref[part] = full[part, group.me]
        query_side(part)

    for part in range(last):
        key_side(part)

    for h in range(HALVES):
        part = slice(h * rows, (h + 1) * rows)
        for cg in range(groups):
            span = slice(cg * width, (cg + 1) * width)
            second(2, h, cg).wait_recv()
            enc_ref[part, span] = unit[h, cg] * gain[:, span] + total(2, h, cg)
    grads_arrive(last)

    for h in range(heads):
        khalo[h].left()
        vhalo[h].left()
    for h in range(HALVES):
        blocks.left(q.at[h], qwindow(h), qs.at[h], qr.at[h])
        blocks.left(do.at[h], dwindow(h), ds_.at[h], dr.at[h])
        blocks.left(drow.at[h], twindow(h), es.at[h], er.at[h])

        @pl.loop(0, groups)
        def _(cg):
            for stage in range(1, 3):
                first(stage, h, cg).wait_send()
                second(stage, h, cg).wait_send()
            for kind in range(3):
                spread(1, full, h, cg, kind).wait_send()
    blocks.left(stat, swindow, ts, tr)


def layer(count, groups, q, k, v, res, w, gain, up, down, cg, source, cot):
    tok, head_cols = q.shape
    model = res.shape[1]
    heads = head_cols // HEAD_DIM
    src = up.shape[1]
    own = tok // groups
    rows, half, width = own // HALVES, tok // HALVES, model // groups
    copies = source.shape[1]
    dma = pltpu.SemaphoreType.DMA
    vm = pl.BlockSpec(memory_space=VM)
    far = pl.BlockSpec(memory_space=pltpu.HBM)
    grad = jax.ShapeDtypeStruct((tok, head_cols), F32)
    scratch = [
        VM(w.shape, BF16), VM(up.shape, BF16), VM(down.shape, BF16), VM((src, copies), BF16),
        VM((own, model), BF16), VM((own, model), BF16),
        VM((1, model), F32), VM((1, copies), F32), VM((1, copies), jnp.int32),
        VM((heads, 5, tok, HEAD_DIM), BF16), VM((heads, 5, tok, HEAD_DIM), BF16),
        VM((HALVES, half, head_cols), BF16), VM((HALVES - 1, 4, half, head_cols), BF16),
        VM((HALVES, half, head_cols), BF16), VM((HALVES - 1, 4, half, head_cols), BF16),
        VM((heads, HALVES, half, 5 * tok), BF16), VM((heads, HALVES - 1, tok, 4 * half), BF16),
        VM((HALVES, half, head_cols), BF16),
        VM((2 * heads, tok), F32), VM((4, 2 * heads, tok), F32),
        VM((HALVES, half, HEAD_DIM), F32), VM((HALVES, 8, half), F32), VM((HALVES - 1, 4, 8, half), F32),
        VM((HALVES, half, src), BF16), VM((HALVES, half, copies), BF16), VM((HALVES, half, src), F32),
        VM((HALVES, half, copies), BF16), VM((half, copies), BF16),
        VM((HALVES, half, src), BF16), VM((half, head_cols), F32),
        VM((8, src), F32),
        VM((HALVES, groups, rows, width), F32), VM((HALVES, rows, HEAD_DIM), F32),
        VM((HALVES, groups, half, width), BF16),
        VM((2, HALVES, groups, 2 * rows, width), BF16),
        VM((2, HALVES, groups, 2 * rows, width), BF16),
        VM((2, HALVES, groups, 2 * rows, width), BF16),
        VM((2, HALVES, groups, rows, width), BF16),
        VM((2, HALVES, groups, rows, width), BF16),
        dma((2 * heads + 7 + PIECES,)), dma((groups * HALVES,)), dma((groups, groups * HALVES)),
        dma((heads, 4)), dma((heads, 4)), dma((heads,)),
        dma((heads, 4)), dma((heads, 4)), dma((heads,)),
        dma((HALVES, 4)), dma((HALVES, 4)), dma((4,)), dma((4,)),
        dma((HALVES, 4)), dma((HALVES, 4)), dma((HALVES, 4)), dma((HALVES, 4)),
        dma((3, HALVES, groups)), dma((3, HALVES, groups)),
        dma((3, HALVES, groups)), dma((3, HALVES, groups)),
        dma((2, HALVES, groups, 3)), dma((2, HALVES, groups, 3)),
    ]
    return pl.pallas_call(
        functools.partial(layer_kernel, count),
        out_shape=(
            jax.ShapeDtypeStruct((own, model), F32),
            jax.ShapeDtypeStruct((HALVES, half, head_cols), F32),
            grad,
            grad,
            jax.ShapeDtypeStruct((HALVES, half, width), BF16),
            jax.ShapeDtypeStruct((heads, tok, HEAD_DIM), BF16),
            jax.ShapeDtypeStruct((4, half, head_cols), BF16),
            jax.ShapeDtypeStruct((4, half, head_cols), BF16),
            jax.ShapeDtypeStruct((4, 8, half), F32),
            jax.ShapeDtypeStruct((heads, tok, 4 * half), BF16),
        ),
        in_specs=[far] * 11,
        out_specs=(vm,) * 10,
        scratch_shapes=scratch,
        compiler_params=pltpu.CompilerParams(
            collective_id=1, has_side_effects=True, vmem_limit_bytes=50855936
        ),
        name="layer",
    )(*[
        pltpu.with_memory_space_constraint(x, pltpu.HBM)
        for x in (q, k, v, res, w, gain, up, down, cg, source, cot)
    ])


def emit_kernel(
    groups, enc, gq, gk, gv, gres, vown, qlast, dlast, tlast, plast,
    enc_out, gq_out, gk_out, gv_out, gres_out, gk_sum, gv_sum, wide, sem, head_sem,
):
    halves, half = gq.shape[:2]
    rows = half // groups
    own = halves * rows
    heads = vown.shape[0]
    copies = [pltpu.make_async_copy(enc, enc_out, sem.at[0])]
    copies[0].start()
    wide[...] = gres[...].astype(F32)
    for i in range(groups * halves):
        owner, h = divmod(i, halves)
        there = pl.ds(owner * own + h * rows, rows)
        here = pl.ds(owner * rows, rows)
        copies.append(
            pltpu.make_async_copy(gq.at[h, here], gq_out.at[there], sem.at[1 + 2 * i])
        )
        copies.append(
            pltpu.make_async_copy(wide.at[h, here], gres_out.at[there], sem.at[2 + 2 * i])
        )
    for copy in copies[1:]:
        copy.start()
    for h in range(heads):
        span = slice(h * HEAD_DIM, (h + 1) * HEAD_DIM)
        queries = qlast[:, :, span].reshape(4 * half, HEAD_DIM)
        grads = dlast[:, :, span].reshape(4 * half, HEAD_DIM)
        delta = jnp.concatenate([tlast[s, h : h + 1, :] for s in range(4)], axis=1)
        chance = plast[h]
        slope = (chance.astype(F32) * (dot_nt(vown[h], grads) - delta)).astype(BF16)
        gv_sum[h] = gv[:, span] + dot_nn(chance, grads)
        gk_sum[h] = gk[:, span] + dot_nn(slope, queries) * SCALE
        there = pl.ds(h * HEAD_DIM, HEAD_DIM)
        outs = [
            pltpu.make_async_copy(gv_sum.at[h], gv_out.at[:, there], head_sem.at[0, h]),
            pltpu.make_async_copy(gk_sum.at[h], gk_out.at[:, there], head_sem.at[1, h]),
        ]
        for copy in outs:
            copy.start()
        copies += outs
    for copy in copies:
        copy.wait()


def emit(groups, enc, gq, gk, gv, gres, vown, *rest):
    halves, half, head_cols = gq.shape
    tok = halves * half
    heads = vown.shape[0]
    grad = jax.ShapeDtypeStruct((tok, head_cols), F32)
    return pl.pallas_call(
        functools.partial(emit_kernel, groups),
        out_shape=(
            jax.ShapeDtypeStruct(enc.shape, F32), grad, grad, grad,
            jax.ShapeDtypeStruct((tok, gres.shape[2]), F32),
        ),
        in_specs=[pl.BlockSpec(memory_space=VM)] * 10,
        out_specs=(pl.BlockSpec(memory_space=pl.ANY),) * 5,
        scratch_shapes=[
            VM((heads, tok, HEAD_DIM), F32),
            VM((heads, tok, HEAD_DIM), F32),
            VM(gres.shape, F32),
            pltpu.SemaphoreType.DMA((1 + 2 * groups * halves,)),
            pltpu.SemaphoreType.DMA((2, heads)),
        ],
        compiler_params=pltpu.CompilerParams(vmem_limit_bytes=24 << 20),
        name="emit",
    )(enc, gq, gk, gv, gres, vown, *rest)


def shards(
    count, groups, query_heads, key_heads, value_heads, residual, out_weight, ln_gain,
    up_source, down_source, copy_gain, neuron_source, cotangent,
):
    parts = layer(
        count, groups, query_heads, key_heads, value_heads, residual, out_weight,
        ln_gain[None, :], up_source, down_source, copy_gain[None, :], neuron_source[None, :],
        cotangent,
    )
    return emit(groups, *parts)


def solution(mesh):
    in_specs = (
        P("seq", "tp"),
        P("seq", "tp"),
        P("seq", "tp"),
        P("seq", None),
        P("tp", None),
        P(),
        P(None, "tp"),
        P("tp", None),
        P("tp"),
        P("tp"),
        P("seq", None),
    )
    out_specs = (
        P(("seq", "tp"), None),
        P("seq", "tp"),
        P("seq", "tp"),
        P("seq", "tp"),
        P("seq", "tp"),
    )
    body = functools.partial(shards, mesh.shape["seq"], mesh.shape["tp"])
    return jax.shard_map(body, mesh=mesh, in_specs=in_specs, out_specs=out_specs, check_vma=False)
```
